32 devices in a mesh: expert: 4 (over z), dp: 8 (over y, x, core).
Axes of the slice: x: 2, y: 2, z: 4, core: 2. Of those that a mesh axis runs over, the one named last changes fastest.
Arguments:
- row_acts: bfloat16 [4, 8192, 2048], P('expert', 'dp'), may hold values from -6 to 6
- row_grads: bfloat16 [4, 8192, 768], P('expert', 'dp'), may hold values from -6 to 6
- grad_factor: bfloat16 [4, 768, 768], P('expert', None, 'dp'), may hold values from -0.21875 to 0.21875
- value_factor: bfloat16 [4, 2048, 768], P('expert', None, 'dp'), may hold values from -0.125 to 0.125
- counts: int32 [4, 8], P('expert', 'dp'), may hold values from 128 to 1024, as said below
- row_token: int32 [4, 8192], P('expert', 'dp'), may hold values from 0 to 1023, as said below
Outputs:
- influence: float32 [8192, 24], P(('expert', 'dp'))
The draws below stay inside these ranges and needn't reach their ends.
Inputs may be any that keep to these rules, and one draw needn't show every extreme that they name: counts[e, b] slots at the start of each block of 1024 slots are live; some block has all 1024 live. `row_token`: within one block of 1024 slots of one expert the ids are distinct, dead slots included.
All inputs are finite; a program needn't handle non-finite values.
Results may differ from the reference program's by a relative error of at most 0.0003.
Values may be sent and summed in bfloat16 or wider, within the bound.
A program may use at most 64 MiB of HBM per device.

```python
import jax
import jax.numpy as jnp
from jax import lax

MODEL = 2048
MOE_FF = 768
RANK = 32
QUERIES = 24
CAP = 1024
TOK_DEV = 256
EXPERTS = 4
ROWS = 8192
TOKENS = 8192


def draw_counts(key, part):
    nblocks = ROWS // CAP
    level_key = jax.random.fold_in(key, 11)
    jitter_key = jax.random.fold_in(key, 12)
    row_key = jax.random.fold_in(key, 13)
    column_key = jax.random.fold_in(key, 14)
    level = jax.random.randint(level_key, (EXPERTS, 1), CAP // 8, CAP + 1)
    jitter = jax.random.randint(jitter_key, (EXPERTS, nblocks), 0, CAP // 4 + 1)
    filled = jnp.minimum(level + jitter, CAP)
    chosen_row = jax.random.randint(row_key, (), 0, EXPERTS)
    chosen_column = jax.random.randint(column_key, (), 0, nblocks)
    row_grid = jnp.arange(EXPERTS, dtype=jnp.int32)[:, None]
    column_grid = jnp.arange(nblocks, dtype=jnp.int32)[None, :]
    marked = (row_grid == chosen_row) & (column_grid == chosen_column)
    return jnp.where(marked, CAP, filled).astype(jnp.int32)


def draw_row_token(key, part):
    nblocks = ROWS // CAP
    shard_tokens = TOK_DEV * EXPERTS
    block_keys = jax.random.split(jax.random.fold_in(key, 21), EXPERTS * nblocks)

    def one_block(block_key):
        return jax.random.permutation(block_key, shard_tokens)[:CAP]
    owner_ids = jax.vmap(one_block)(block_keys)
    return owner_ids.reshape(EXPERTS, ROWS).astype(jnp.int32)


def shard_levels(stream_key, dims, pieces, low, high):
    level, own = 1.0, jax.random.fold_in(stream_key, 6)
    for position, parts in pieces:
        draws = jnp.exp(jax.random.uniform(jax.random.fold_in(own, position), (parts,), jnp.float32, low / len(pieces), high / len(pieces)))
        level = level * jnp.repeat(draws, dims[position] // parts).reshape([-1 if axis == position else 1 for axis in range(len(dims))])
    return level


def normal_values(key, shape, spread, limit, pieces=(), kind=jnp.bfloat16):
    values = jax.random.normal(key, shape, jnp.float32) * spread
    if len(pieces) > 0:
        values = shard_levels(key, shape, pieces, -0.22, 0.18) * values
    return jnp.clip(values, min=-limit, max=limit).astype(kind)


def setup_inputs(seed: int = 0) -> dict:
    seeds = jax.random.split(jax.random.key(seed), 7)
    row_acts = normal_values(seeds[0], (EXPERTS, ROWS, MODEL), 1.0, 6.0, ((0, 4), (1, 8)))
    row_grads = normal_values(seeds[1], (EXPERTS, ROWS, MOE_FF), 1.0, 6.0, ((0, 4), (1, 8)))
    grad_factor = normal_values(seeds[2], (EXPERTS, MOE_FF, QUERIES * RANK), MOE_FF ** -0.5, 0.21875, ((0, 4), (2, 8)))
    value_factor = normal_values(seeds[3], (EXPERTS, MODEL, QUERIES * RANK), MODEL ** -0.5, 0.125, ((0, 4), (2, 8)))
    counts = draw_counts(jax.random.fold_in(seeds[6], 71), 0)
    row_token = draw_row_token(jax.random.fold_in(seeds[6], 71), 0)
    return dict(row_acts=row_acts, row_grads=row_grads, grad_factor=grad_factor, value_factor=value_factor, counts=counts, row_token=row_token)


epsilon = 1e-06

def reference(row_acts, row_grads, grad_factor, value_factor, counts, row_token):
    nblocks = ROWS // CAP
    shard_tokens = TOK_DEV * EXPERTS
    column_ids = jnp.arange(QUERIES * RANK, dtype=jnp.int32)[:, None] // RANK
    query_ids = jnp.arange(QUERIES, dtype=jnp.int32)[None, :]
    grouping = (column_ids == query_ids).astype(jnp.float32)
    slot_ids = jnp.arange(CAP, dtype=jnp.int32)

    def one_block(block_id):

        def one_expert(carry, expert_id):
            total_now, norm_now = carry
            start = (block_id * CAP).astype(jnp.int32)
            activ = lax.dynamic_slice(row_acts, (expert_id, start, jnp.int32(0)), (1, CAP, MODEL))[0]
            gradient = lax.dynamic_slice(row_grads, (expert_id, start, jnp.int32(0)), (1, CAP, MOE_FF))[0]
            acts_proj = jnp.dot(activ, value_factor[expert_id], preferred_element_type=jnp.float32)
            grads_proj = jnp.dot(gradient, grad_factor[expert_id], preferred_element_type=jnp.float32)
            scores = jnp.dot(acts_proj * grads_proj, grouping, precision=lax.Precision.HIGHEST)
            live = (slot_ids < counts[expert_id, block_id]).astype(jnp.float32)
            norms = lax.optimization_barrier(jnp.sum(jnp.square(activ.astype(jnp.float32)), 1)) * lax.optimization_barrier(jnp.sum(jnp.square(gradient.astype(jnp.float32)), 1))
            owner_ids = lax.dynamic_slice(row_token, (expert_id, start), (1, CAP))[0]
            total_now = total_now.at[owner_ids].add(scores * live[:, None])
            norm_now = norm_now.at[owner_ids].add(norms * live)
            return ((total_now, norm_now), None)
        start_carry = (jnp.zeros((shard_tokens, QUERIES), jnp.float32), jnp.zeros((shard_tokens,), jnp.float32))
        (total_now, norm_now), _ = lax.scan(one_expert, start_carry, jnp.arange(EXPERTS, dtype=jnp.int32))
        return (total_now, norm_now)
    totals, norm_sum = lax.map(one_block, jnp.arange(nblocks, dtype=jnp.int32))
    factor = lax.rsqrt(norm_sum / (MODEL * MOE_FF) + epsilon) / jnp.sqrt(jnp.float32(RANK))
    result = totals * factor[..., None]
    result = result.reshape(nblocks, EXPERTS, TOK_DEV, QUERIES).transpose(1, 0, 2, 3)
    return result.reshape(TOKENS, QUERIES)
```

```python
import functools

import jax
import jax.numpy as jnp
from jax import lax
from jax.experimental import pallas as pl
from jax.experimental.pallas import tpu as pltpu
from jax.sharding import PartitionSpec as P

RANK = 32
TOK_DEV = 256
LANES = 128
PACK = 16
V_PARTS = (2, 4, 8, 8)

epsilon = 1e-06
MESH = pl.DeviceIdType.MESH
CONTRACT_LAST = (((1,), (1,)), ((), ()))


def round_up(value, unit):
    return -(-value // unit) * unit


def kernel(
    dims,
    count_ref,
    token_hbm,
    acts_hbm,
    grads_hbm,
    gfac_hbm,
    vfac_hbm,
    out_ref,
    tokens,
    acts,
    grads,
    gfac,
    vfac,
    gproj,
    aproj,
    scores,
    far_scores,
    onehot,
    dense,
    landed,
    far_dense,
    far_landed,
    load_sem,
    send_sem,
    recv_sem,
    zsend_sem,
    zrecv_sem,
):
    n_dp, n_exp, across, queries, real_cols, granule = dims
    chips = n_dp // 2
    half = chips // 2
    rows, model = acts.shape
    cols = gfac.shape[2]
    me_e = lax.axis_index("expert")
    me = lax.axis_index("dp")
    core = me % 2
    other = 1 - core

    def walk(index):
        line, at = index // across, index % across
        back = line % 2
        return line * across + at + back * (across - 1 - 2 * at)

    place = walk(me // 2)

    def chip_at(step):
        return walk((place + step + chips) % chips)

    mine = chip_at(0)
    ahead = chip_at(1) * 2 + core
    behind = chip_at(-1) * 2 + core
    partner = mine * 2 + other

    pieces, start = [None], 0
    for part in V_PARTS:
        pieces.append(pl.ds(start, model // part))
        start += model // part
    last_piece = len(pieces) - 1

    def held(chip, side, piece):
        if pieces[piece] is None:
            return gfac.at[chip, side]
        return vfac.at[chip, side, :, pieces[piece]]

    def own(piece):
        if pieces[piece] is None:
            return gfac_hbm
        return vfac_hbm.at[:, pieces[piece]]

    sent = []

    def send(src, chip, side, piece, target):
        copy = pltpu.make_async_remote_copy(
            src_ref=src,
            dst_ref=held(chip, side, piece),
            send_sem=send_sem.at[len(sent)],
            recv_sem=recv_sem.at[chip, side, piece],
            device_id=(me_e, target),
            device_id_type=MESH,
        )
        copy.start()
        sent.append(copy)

    def arrived(chip, side, piece):
        pltpu.make_async_remote_copy(
            src_ref=held(chip, side, piece),
            dst_ref=held(chip, side, piece),
            send_sem=send_sem.at[0],
            recv_sem=recv_sem.at[chip, side, piece],
            device_id=(me_e, partner),
            device_id_type=MESH,
        ).wait_recv()

    barrier = pltpu.get_barrier_semaphore()
    for target in (ahead, behind, partner):
        pl.semaphore_signal(barrier, inc=1, device_id=(me_e, target), device_id_type=MESH)
    for i in range(1, n_exp):
        pl.semaphore_signal(
            barrier, inc=1, device_id=((me_e + i) % n_exp, me), device_id_type=MESH
        )

    n_pieces = len(pieces)
    load_tokens = pltpu.make_async_copy(token_hbm, tokens, load_sem.at[n_pieces + 2])
    load_tokens.start()
    loads = [
        pltpu.make_async_copy(own(j), held(mine, core, j), load_sem.at[j])
        for j in range(n_pieces)
    ]
    load_grads = pltpu.make_async_copy(grads_hbm, grads, load_sem.at[n_pieces])
    load_acts = pltpu.make_async_copy(acts_hbm, acts, load_sem.at[n_pieces + 1])
    for copy in loads:
        copy.start()
    load_grads.start()
    load_acts.start()
    with jax.named_scope("barrier"):
        pl.semaphore_wait(barrier, 3 + n_exp - 1)

    for j in range(n_pieces):
        send(own(j), mine, core, j, ahead)
        send(own(j), mine, core, j, behind)
        send(own(j), mine, core, j, partner)

    with jax.named_scope("onehot"):
        load_tokens.wait()
        slot_ids = lax.broadcasted_iota(jnp.int32, (1, rows), 1)
        names = jnp.where(slot_ids < count_ref[0, 0], tokens[...], -1)
        names = jnp.broadcast_to(names, (LANES, rows)).T
        lane_ids = lax.broadcasted_iota(jnp.int32, (rows, LANES), 1)
        for i in range(n_exp * TOK_DEV // LANES):
            hit = (names == lane_ids + i * LANES).astype(jnp.float32)
            onehot[:, i * LANES : (i + 1) * LANES] = hit.astype(onehot.dtype)

    with jax.named_scope("loadwait"):
        load_grads.wait()
        load_acts.wait()

    def energy(ref):
        total = jnp.zeros((rows, LANES), jnp.float32)
        for i in range(ref.shape[1] // LANES):
            part = ref[:, i * LANES : (i + 1) * LANES].astype(jnp.float32)
            total = total + part * part
        return jnp.sum(total.T, axis=0, keepdims=True)

    with jax.named_scope("energy"):
        scores[...] = jnp.zeros_like(scores)
        far_scores[...] = jnp.zeros_like(far_scores)
        scores[queries : queries + 1] = energy(acts) * energy(grads)

    def project(factors, ref, span):
        factor = [f.reshape(2 * cols, f.shape[-1]) for f in factors]
        factor = jnp.concatenate(factor, axis=0) if len(factor) > 1 else factor[0]
        return lax.dot_general(
            factor, ref[:, span], CONTRACT_LAST, preferred_element_type=jnp.float32
        ).reshape(len(factors), 2, cols, rows)

    def project_grads(sources):
        gproj[: len(sources)] = project(
            [gfac[chip] for chip in sources], grads, pl.ds(0, grads.shape[1])
        )

    def project_acts(sources, span):
        return project([vfac[chip, :, :, span] for chip in sources], acts, span)

    def score(target, first, chip, side, product):
        for i in range(real_cols // granule):
            query = ((2 * chip + side) * real_cols + i * granule) // RANK - first
            part = product[i * granule : (i + 1) * granule]
            target[pl.ds(query, 1)] += jnp.sum(part, axis=0, keepdims=True)

    def owner_at(k):
        low = k + (k >= me_e).astype(jnp.int32)
        high = n_exp - 1 - k
        high = high - (high <= me_e).astype(jnp.int32)
        return jnp.where(2 * me_e < n_exp, high, low)

    def of_owner(owner):
        return pl.ds(pl.multiple_of(owner * TOK_DEV, TOK_DEV), TOK_DEV)

    def hand_over(total, stage, own_sums, others):
        depth = total.shape[0]
        high = total.astype(jnp.bfloat16).astype(jnp.float32)
        both = jnp.concatenate([high, total - high], axis=0).astype(jnp.bfloat16)

        def tokens_of(owner):
            sums = jnp.dot(
                both, onehot[:, of_owner(owner)], preferred_element_type=jnp.float32
            )
            own_sums[owner] = sums[:depth] + sums[depth:]

        copies = []
        for k in range(n_exp - 1):
            owner = owner_at(k)
            tokens_of(owner)
            copy = pltpu.make_async_remote_copy(
                src_ref=own_sums.at[owner],
                dst_ref=others.at[me_e],
                send_sem=zsend_sem.at[stage, k],
                recv_sem=zrecv_sem.at[stage, me_e],
                device_id=(owner, me),
                device_id_type=MESH,
            )
            copy.start()
            copies.append(copy)
        tokens_of(me_e)
        return copies

    def collect(stage, own_sums, others):
        result = own_sums[me_e]
        for k in reversed(range(n_exp - 1)):
            source = owner_at(k)
            pltpu.make_async_remote_copy(
                src_ref=own_sums.at[source],
                dst_ref=others.at[source],
                send_sem=zsend_sem.at[stage, k],
                recv_sem=zrecv_sem.at[stage, source],
                device_id=(source, me),
                device_id_type=MESH,
            ).wait_recv()
            result = result + others[source]
        return result

    with jax.named_scope("mine"):
        for j in range(n_pieces):
            loads[j].wait()
            arrived(mine, other, j)
            if j == 0:
                project_grads([mine])
        product = project_acts([mine], pl.ds(0, model))[0] * gproj[0]
        for side in range(2):
            score(scores, 0, mine, side, product[side])

    def sources_of(step):
        return [chip_at(-step)] if step == half else [chip_at(-step), chip_at(step)]

    def pass_on(step, j):
        sources = sources_of(step)
        for chip in sources:
            arrived(chip, core, j)
            send(held(chip, core, j), chip, core, j, partner)
        if step < half - 1:
            send(held(sources[0], core, j), sources[0], core, j, ahead)
            send(held(sources[1], core, j), sources[1], core, j, behind)
        elif step == half - 1:
            chip = chip_at(step * (2 * core - 1))
            target = chip_at(1 - 2 * core) * 2 + core
            send(held(chip, core, j), chip, core, j, target)

    far_chip = chip_at(half)
    base = 2 * far_chip * real_cols // RANK

    def multiply(step, j):
        sources = sources_of(step)
        for chip in sources:
            arrived(chip, other, j)
        count = len(sources)
        if j == 0:
            project_grads(sources)
        elif j == 1:
            aproj[:count] = project_acts(sources, pieces[j])
        elif j < last_piece:
            aproj[:count] += project_acts(sources, pieces[j])
        else:
            product = (aproj[:count] + project_acts(sources, pieces[j])) * gproj[:count]
            for buf, chip in enumerate(sources):
                for side in range(2):
                    if step == half:
                        score(far_scores, base, chip, side, product[buf, side])
                    else:
                        score(scores, 0, chip, side, product[buf, side])

    order = [(step, j) for step in range(1, half + 1) for j in range(n_pieces)]
    near = None
    for at, event in enumerate(order):
        with jax.named_scope(f"pass{event[0]}{event[1]}"):
            pass_on(*event)
        if at:
            with jax.named_scope(f"mul{order[at - 1][0]}{order[at - 1][1]}"):
                multiply(*order[at - 1])
        if event == (half, 0):
            with jax.named_scope("near"):
                near = hand_over(scores[...], 0, dense, landed)
    with jax.named_scope("mullast"):
        multiply(*order[-1])

    with jax.named_scope("far"):
        far = hand_over(far_scores[...], 1, far_dense, far_landed)
    with jax.named_scope("colnear"):
        result = collect(0, dense, landed)
        factor = lax.rsqrt(
            result[queries : queries + 1] / (model * grads.shape[1]) + epsilon
        )
        factor = factor / jnp.sqrt(jnp.float32(RANK))
    with jax.named_scope("colfar"):
        late = collect(1, far_dense, far_landed)
    row_ids = lax.broadcasted_iota(jnp.int32, result.shape, 0)
    for i in range(late.shape[0]):
        result = result + jnp.where(row_ids == base + i, late[i : i + 1], 0.0)
    out_ref[...] = result[:queries] * factor
    with jax.named_scope("sends"):
        for copy in near + far + sent:
            copy.wait_send()


def local(dims, row_acts, row_grads, grad_factor, value_factor, counts, row_token):
    n_dp, n_exp, across, queries, real_cols, granule = dims
    gfac, vfac = grad_factor[0].T, value_factor[0].T
    cols = round_up(real_cols, PACK)
    if cols != real_cols:
        pad = ((0, cols - real_cols), (0, 0))
        gfac, vfac = jnp.pad(gfac, pad), jnp.pad(vfac, pad)
    rows, model = row_acts.shape[1:]
    units = row_grads.shape[2]
    chips = n_dp // 2
    depth = round_up(queries + 1, 8)
    n_pieces = 1 + len(V_PARTS)
    few = round_up((2 * real_cols - 1) // RANK + 2, 8)
    bufs = 2
    n_sends = n_pieces * (3 + sum(
        (1 if s == chips // 2 else 3 if s == chips // 2 - 1 else 4)
        for s in range(1, chips // 2 + 1)
    ))
    any_space = pl.BlockSpec(memory_space=pl.ANY)
    turned = pl.pallas_call(
        functools.partial(kernel, dims),
        name="influence_exchange",
        out_shape=pltpu.VMEM((queries, TOK_DEV), jnp.float32),
        in_specs=[pl.BlockSpec(memory_space=pltpu.SMEM)] + [any_space] * 5,
        out_specs=pl.BlockSpec(memory_space=pltpu.VMEM),
        scratch_shapes=[
            pltpu.VMEM((1, rows), jnp.int32),
            pltpu.VMEM((rows, model), jnp.bfloat16),
            pltpu.VMEM((rows, units), jnp.bfloat16),
            pltpu.VMEM((chips, 2, cols, units), jnp.bfloat16),
            pltpu.VMEM((chips, 2, cols, model), jnp.bfloat16),
            pltpu.VMEM((bufs, 2, cols, rows), jnp.float32),
            pltpu.VMEM((bufs, 2, cols, rows), jnp.float32),
            pltpu.VMEM((depth, rows), jnp.float32),
            pltpu.VMEM((few, rows), jnp.float32),
            pltpu.VMEM((rows, n_exp * TOK_DEV), jnp.bfloat16),
            pltpu.VMEM((n_exp, depth, TOK_DEV), jnp.float32),
            pltpu.VMEM((n_exp, depth, TOK_DEV), jnp.float32),
            pltpu.VMEM((n_exp, few, TOK_DEV), jnp.float32),
            pltpu.VMEM((n_exp, few, TOK_DEV), jnp.float32),
            pltpu.SemaphoreType.DMA((n_pieces + 3,)),
            pltpu.SemaphoreType.DMA((n_sends,)),
            pltpu.SemaphoreType.DMA((chips, 2, n_pieces)),
            pltpu.SemaphoreType.DMA((2, n_exp - 1)),
            pltpu.SemaphoreType.DMA((2, n_exp)),
        ],
        compiler_params=pltpu.CompilerParams(
            collective_id=0, has_side_effects=True, vmem_limit_bytes=60 * 1024 * 1024
        ),
    )(counts, row_token, row_acts[0], row_grads[0], gfac, vfac)
    return turned.T


def solution(mesh):
    n_exp, n_dp = mesh.shape["expert"], mesh.shape["dp"]
    across = len({d.coords[0] for d in mesh.devices.flat})

    def whole(row_acts, row_grads, grad_factor, value_factor, counts, row_token):
        all_cols = grad_factor.shape[2]
        real_cols = all_cols // n_dp
        granule = real_cols if RANK % real_cols == 0 else RANK
        while real_cols % granule:
            granule //= 2
        dims = (n_dp, n_exp, across, all_cols // RANK, real_cols, granule)
        return jax.shard_map(
            functools.partial(local, dims),
            mesh=mesh,
            in_specs=(
                P("expert", "dp", None),
                P("expert", "dp", None),
                P("expert", None, "dp"),
                P("expert", None, "dp"),
                P("expert", "dp"),
                P("expert", "dp"),
            ),
            out_specs=P(("expert", "dp"), None),
            check_vma=False,
        )(row_acts, row_grads, grad_factor, value_factor, counts, row_token)

    return whole
```

```python
import functools

import jax
import jax.numpy as jnp
from jax import lax
from jax.experimental import pallas as pl
from jax.experimental.pallas import tpu as pltpu
from jax.sharding import PartitionSpec as P

RANK = 32
TOK_DEV = 256
LANES = 128
PACK = 16
V_PARTS = (2, 4, 8, 8)
CHUNK = 256
CHUNKS_BEFORE_RELAY = 8

epsilon = 1e-06
MESH = pl.DeviceIdType.MESH
CONTRACT_LAST = (((1,), (1,)), ((), ()))


def round_up(value, unit):
    return -(-value // unit) * unit


def kernel(
    dims,
    count_ref,
    token_hbm,
    acts_hbm,
    grads_hbm,
    gfac_hbm,
    vfac_hbm,
    out_ref,
    tokens,
    rows,
    by_token,
    fac,
    gproj,
    aproj,
    scores,
    onehot,
    energies,
    landed,
    far_dense,
    far_landed,
    load_sem,
    send_sem,
    own_sem,
    direct_sem,
    relay_sem,
    zsend_sem,
    zrecv_sem,
):
    n_dp, n_exp, across, queries, real_cols, granule, units = dims
    chips = n_dp // 2
    half = chips // 2
    slots, width = rows.shape
    model = width - units
    n_tok = by_token.shape[0]
    cols = fac.shape[1]
    me_e = lax.axis_index("expert")
    me = lax.axis_index("dp")
    core = me % 2
    other = 1 - core

    def walk(index):
        line, at = index // across, index % across
        back = line % 2
        return line * across + at + back * (across - 1 - 2 * at)

    place = walk(me // 2)

    def chip_at(step):
        return walk((place + step + chips) % chips)

    mine = chip_at(0)
    ahead = chip_at(1) * 2 + core
    behind = chip_at(-1) * 2 + core
    partner = mine * 2 + other

    pieces, start = [pl.ds(0, units)], units
    for part in V_PARTS:
        pieces.append(pl.ds(start, model // part))
        start += model // part
    n_pieces = len(pieces)
    last_piece = n_pieces - 1

    def own(j):
        if j == 0:
            return gfac_hbm
        return vfac_hbm.at[:, pl.ds(pieces[j].start - units, pieces[j].size)]

    sent = []

    def send(src, dst, sem, target):
        copy = pltpu.make_async_remote_copy(
            src_ref=src,
            dst_ref=dst,
            send_sem=send_sem.at[0],
            recv_sem=sem,
            device_id=(me_e, target),
            device_id_type=MESH,
        )
        copy.start()
        sent.append(src.shape[0] * src.shape[1])

    def wait_for(ref, sem):
        pltpu.make_async_remote_copy(
            src_ref=ref,
            dst_ref=ref,
            send_sem=send_sem.at[0],
            recv_sem=sem,
            device_id=(me_e, partner),
            device_id_type=MESH,
        ).wait_recv()

    barrier = pltpu.get_barrier_semaphore()
    for target in (ahead, behind, partner):
        pl.semaphore_signal(barrier, inc=1, device_id=(me_e, target), device_id_type=MESH)
    for i in range(1, n_exp):
        pl.semaphore_signal(
            barrier, inc=1, device_id=((me_e + i) % n_exp, me), device_id_type=MESH
        )

    g_span, v_span = pl.ds(0, units), pl.ds(units, model)
    own_slot = mine * 2 + core
    load_tokens = pltpu.make_async_copy(token_hbm, tokens, load_sem.at[0])
    load_tokens.start()
    pltpu.make_async_copy(grads_hbm, rows.at[:, g_span], load_sem.at[1]).start()
    pltpu.make_async_copy(acts_hbm, rows.at[:, v_span], load_sem.at[1]).start()
    pltpu.make_async_copy(gfac_hbm, fac.at[own_slot, :, g_span], load_sem.at[2]).start()
    pltpu.make_async_copy(vfac_hbm, fac.at[own_slot, :, v_span], load_sem.at[2]).start()
    with jax.named_scope("barrier"):
        pl.semaphore_wait(barrier, 3 + n_exp - 1)

    for j in range(n_pieces):
        for target in (ahead, behind):
            send(own(j), fac.at[own_slot, :, pieces[j]], direct_sem.at[0, j], target)
    send(gfac_hbm, fac.at[own_slot, :, g_span], own_sem.at[0], partner)
    send(vfac_hbm, fac.at[own_slot, :, v_span], own_sem.at[0], partner)

    with jax.named_scope("onehot"):
        load_tokens.wait()
        slot_ids = lax.broadcasted_iota(jnp.int32, (1, slots), 1)
        names = jnp.where(slot_ids < count_ref[0, 0], tokens[...], -1)
        token_ids = lax.broadcasted_iota(jnp.int32, onehot.shape, 0)
        onehot[...] = (token_ids == names).astype(jnp.float32).astype(onehot.dtype)
        scores[...] = jnp.zeros_like(scores)
        far_dense[...] = jnp.zeros_like(far_dense)
        energies[...] = jnp.zeros_like(energies)

    with jax.named_scope("loadwait"):
        pltpu.make_async_copy(rows, rows, load_sem.at[1]).wait()

    def order_rows(first, size):
        part = jnp.dot(
            onehot[...], rows[:, first : first + size], preferred_element_type=jnp.float32
        )
        by_token[:, first : first + size] = part.astype(by_token.dtype)
        kind = int(first >= units)
        squares = part * part
        for i in range(size // LANES):
            energies[kind] += squares[:, i * LANES : (i + 1) * LANES]

    chunks = [(i, CHUNK) for i in range(0, width, CHUNK)]

    def project(factor, ref, span):
        return lax.dot_general(
            factor, ref[:, span], CONTRACT_LAST, preferred_element_type=jnp.float32
        )

    def project_pair(sources, span):
        factor = [fac[pl.ds(2 * chip, 2), :, span] for chip in sources]
        factor = jnp.concatenate([f.reshape(2 * cols, span.size) for f in factor], axis=0)
        return project(factor, by_token, span).reshape(len(sources), 2, cols, n_tok)

    def group_sums(chip, side, product):
        for i in range(real_cols // granule):
            query = ((2 * chip + side) * real_cols + i * granule) // RANK
            part = product[i * granule : (i + 1) * granule]
            yield query, jnp.sum(part, axis=0, keepdims=True)

    def owner_at(k):
        low = k + (k >= me_e).astype(jnp.int32)
        high = n_exp - 1 - k
        high = high - (high <= me_e).astype(jnp.int32)
        return jnp.where(2 * me_e < n_exp, high, low)

    def of_owner(owner):
        return pl.ds(pl.multiple_of(owner * TOK_DEV, TOK_DEV), TOK_DEV)

    def hand_over(stage, src, dst, owner):
        pltpu.make_async_remote_copy(
            src_ref=src,
            dst_ref=dst,
            send_sem=zsend_sem.at[stage],
            recv_sem=zrecv_sem.at[stage],
            device_id=(owner, me),
            device_id_type=MESH,
        ).start()

    def handed(stage, ref):
        all_of = ref.at[pl.ds(0, n_exp - 1)]
        return pltpu.make_async_remote_copy(
            src_ref=all_of,
            dst_ref=all_of,
            send_sem=zsend_sem.at[stage],
            recv_sem=zrecv_sem.at[stage],
            device_id=((me_e + 1) % n_exp, me),
            device_id_type=MESH,
        )

    def sources_of(step):
        return [chip_at(-step)] if step == half else [chip_at(-step), chip_at(step)]

    def pass_on(step, j):
        sources = sources_of(step)
        count = len(sources)
        span = pieces[j]
        wait_for(fac.at[pl.ds(0, count), :, span], direct_sem.at[step - 1, j])

        def relay(chip, sem, target):
            part = fac.at[2 * chip + core, :, span]
            send(part, part, sem, target)

        if step < half - 1:
            relay(sources[0], direct_sem.at[step, j], ahead)
            relay(sources[1], direct_sem.at[step, j], behind)
        elif step == half - 1:
            chip = chip_at(step * (2 * core - 1))
            target = chip_at(1 - 2 * core) * 2 + core
            relay(chip, direct_sem.at[step, j], target)
        for chip in sources:
            relay(chip, relay_sem.at[step - 1, j], partner)

    def relayed(step, j):
        count = len(sources_of(step))
        wait_for(fac.at[pl.ds(0, count), :, pieces[j]], relay_sem.at[step - 1, j])

    far_chip = chip_at(half)
    base = 2 * far_chip * real_cols // RANK

    def multiply(step, j):
        sources = sources_of(step)
        count = len(sources)
        relayed(step, j)
        value = project_pair(sources, pieces[j])
        if j == 0:
            gproj[:count] = value
        elif j == 1:
            aproj[:count] = value
        elif j < last_piece:
            aproj[:count] += value
        else:
            product = (aproj[:count] + value) * gproj[:count]
            for buf, chip in enumerate(sources):
                for side in range(2):
                    for query, total in group_sums(chip, side, product[buf, side]):
                        scores[pl.ds(query, 1)] += total

    with jax.named_scope("perm"):
        for chunk in chunks[:CHUNKS_BEFORE_RELAY]:
            order_rows(*chunk)
    with jax.named_scope("pass10"):
        pass_on(1, 0)
    with jax.named_scope("perm2"):
        for chunk in chunks[CHUNKS_BEFORE_RELAY:]:
            order_rows(*chunk)
    with jax.named_scope("energy"):
        totals = [
            jnp.sum(energies[kind].T, axis=0, keepdims=True) for kind in range(2)
        ]
        scores[queries : queries + 1] = totals[0] * totals[1]

    with jax.named_scope("mine"):
        own_shard = fac.at[own_slot]
        pltpu.make_async_copy(own_shard, own_shard, load_sem.at[2]).wait()
        wait_for(own_shard, own_sem.at[0])
        product = project_pair([mine], v_span)[0] * project_pair([mine], g_span)[0]
        for side in range(2):
            for query, total in group_sums(mine, side, product[side]):
                scores[pl.ds(query, 1)] += total

    order = [(step, j) for step in range(1, half + 1) for j in range(n_pieces)]
    for at, event in enumerate(order):
        if not at:
            continue
        with jax.named_scope(f"pass{event[0]}{event[1]}"):
            pass_on(*event)
        with jax.named_scope(f"mul{order[at - 1][0]}{order[at - 1][1]}"):
            multiply(*order[at - 1])
        if event == (half, 0):
            with jax.named_scope("near"):
                for k in range(n_exp - 1):
                    owner = owner_at(k)
                    hand_over(0, scores.at[:, of_owner(owner)], landed.at[me_e], owner)

    def far_sums(side, owner, product):
        for query, total in group_sums(far_chip, side, product):
            far_dense[owner, pl.ds(query - base, 1)] += total

    span = pieces[last_piece]
    with jax.named_scope("ownhalf"):
        value = project(fac[2 * far_chip + core, :, span], by_token, span)
        product = (aproj[0, core] + value) * gproj[0, core]
        for owner in range(n_exp):
            far_sums(core, owner, product[:, owner * TOK_DEV : (owner + 1) * TOK_DEV])
    with jax.named_scope("lastrelay"):
        relayed(half, last_piece)
    with jax.named_scope("far"):
        for k in range(n_exp):
            owner = owner_at(k) if k < n_exp - 1 else me_e
            tok = of_owner(owner)
            value = lax.dot_general(
                fac[2 * far_chip + other, :, span],
                by_token[tok, span],
                CONTRACT_LAST,
                preferred_element_type=jnp.float32,
            )
            far_sums(other, owner, (aproj[0, other, :, tok] + value) * gproj[0, other, :, tok])
            if k < n_exp - 1:
                hand_over(1, far_dense.at[owner], far_landed.at[me_e], owner)

    near_wait, far_wait = handed(0, landed), handed(1, far_landed)
    with jax.named_scope("colnear"):
        result = scores[:, of_owner(me_e)]
        near_wait.wait_recv()
        for k in range(n_exp - 1):
            result = result + landed[owner_at(k)]
        factor = lax.rsqrt(result[queries : queries + 1] / (model * units) + epsilon)
        factor = factor / jnp.sqrt(jnp.float32(RANK))
        late = far_dense[me_e]
    with jax.named_scope("colfar"):
        far_wait.wait_recv()
    for k in range(n_exp - 1):
        late = late + far_landed[owner_at(k)]
    row_ids = lax.broadcasted_iota(jnp.int32, result.shape, 0)
    for i in range(late.shape[0]):
        result = result + jnp.where(row_ids == base + i, late[i : i + 1], 0.0)
    out_ref[...] = result[:queries] * factor
    with jax.named_scope("sends"):
        near_wait.wait_send()
        far_wait.wait_send()
        all_sent = fac.at[pl.ds(0, sum(sent) // (cols * width))]
        pltpu.make_async_remote_copy(
            src_ref=all_sent,
            dst_ref=all_sent,
            send_sem=send_sem.at[0],
            recv_sem=own_sem.at[0],
            device_id=(me_e, partner),
            device_id_type=MESH,
        ).wait_send()


def local(dims, row_acts, row_grads, grad_factor, value_factor, counts, row_token):
    n_dp, n_exp, across, queries, real_cols, granule = dims
    gfac, vfac = grad_factor[0].T, value_factor[0].T
    cols = round_up(real_cols, PACK)
    if cols != real_cols:
        pad = ((0, cols - real_cols), (0, 0))
        gfac, vfac = jnp.pad(gfac, pad), jnp.pad(vfac, pad)
    slots, model = row_acts.shape[1:]
    units = row_grads.shape[2]
    width = units + model
    chips = n_dp // 2
    steps = chips // 2
    depth = round_up(queries + 1, 8)
    n_tok = n_exp * TOK_DEV
    n_pieces = 1 + len(V_PARTS)
    few = round_up((2 * real_cols - 1) // RANK + 2, 8)
    any_space = pl.BlockSpec(memory_space=pl.ANY)
    turned = pl.pallas_call(
        functools.partial(kernel, (*dims, units)),
        name="influence_exchange",
        out_shape=pltpu.VMEM((queries, TOK_DEV), jnp.float32),
        in_specs=[pl.BlockSpec(memory_space=pltpu.SMEM)] + [any_space] * 5,
        out_specs=pl.BlockSpec(memory_space=pltpu.VMEM),
        scratch_shapes=[
            pltpu.VMEM((1, slots), jnp.int32),
            pltpu.VMEM((slots, width), jnp.bfloat16),
            pltpu.VMEM((n_tok, width), jnp.bfloat16),
            pltpu.VMEM((n_dp, cols, width), jnp.bfloat16),
            pltpu.VMEM((2, 2, cols, n_tok), jnp.float32),
            pltpu.VMEM((2, 2, cols, n_tok), jnp.float32),
            pltpu.VMEM((depth, n_tok), jnp.float32),
            pltpu.VMEM((n_tok, slots), jnp.bfloat16),
            pltpu.VMEM((2, n_tok, LANES), jnp.float32),
            pltpu.VMEM((n_exp, depth, TOK_DEV), jnp.float32),
            pltpu.VMEM((n_exp, few, TOK_DEV), jnp.float32),
            pltpu.VMEM((n_exp, few, TOK_DEV), jnp.float32),
            pltpu.SemaphoreType.DMA((3,)),
            pltpu.SemaphoreType.DMA((1,)),
            pltpu.SemaphoreType.DMA((1,)),
            pltpu.SemaphoreType.DMA((steps, n_pieces)),
            pltpu.SemaphoreType.DMA((steps, n_pieces)),
            pltpu.SemaphoreType.DMA((2,)),
            pltpu.SemaphoreType.DMA((2,)),
        ],
        compiler_params=pltpu.CompilerParams(
            collective_id=0, has_side_effects=True, vmem_limit_bytes=60 * 1024 * 1024
        ),
    )(counts, row_token, row_acts[0], row_grads[0], gfac, vfac)
    return turned.T


def solution(mesh):
    n_exp, n_dp = mesh.shape["expert"], mesh.shape["dp"]
    across = len({d.coords[0] for d in mesh.devices.flat})

    def whole(row_acts, row_grads, grad_factor, value_factor, counts, row_token):
        all_cols = grad_factor.shape[2]
        real_cols = all_cols // n_dp
        granule = real_cols if RANK % real_cols == 0 else RANK
        while real_cols % granule:
            granule //= 2
        dims = (n_dp, n_exp, across, all_cols // RANK, real_cols, granule)
        return jax.shard_map(
            functools.partial(local, dims),
            mesh=mesh,
            in_specs=(
                P("expert", "dp", None),
                P("expert", "dp", None),
                P("expert", None, "dp"),
                P("expert", None, "dp"),
                P("expert", "dp"),
                P("expert", "dp"),
            ),
            out_specs=P(("expert", "dp"), None),
            check_vma=False,
        )(row_acts, row_grads, grad_factor, value_factor, counts, row_token)

    return whole
```

```python
import functools

import jax
import jax.numpy as jnp
from jax import lax
from jax.experimental import pallas as pl
from jax.experimental.pallas import tpu as pltpu
from jax.sharding import PartitionSpec as P

RANK = 32
TOK_DEV = 256
LANES = 128
PACK = 16
V_EIGHTHS = (3, 2, 2, 1)
CHUNK = 256
CHUNKS_BEFORE_RELAY = 8

epsilon = 1e-06
MESH = pl.DeviceIdType.MESH
CONTRACT_LAST = (((1,), (1,)), ((), ()))


def round_up(value, unit):
    return -(-value // unit) * unit


def kernel(
    dims,
    count_ref,
    token_hbm,
    acts_hbm,
    grads_hbm,
    gfac_hbm,
    vfac_hbm,
    out_ref,
    tokens,
    rows,
    by_token,
    mate,
    fac,
    gproj,
    aproj,
    edge_g,
    edge_a,
    scores,
    onehot,
    energies,
    landed,
    far_dense,
    far_landed,
    load_sem,
    send_sem,
    own_sem,
    direct_sem,
    relay_sem,
    mate_sem,
    zsend_sem,
    zrecv_sem,
):
    n_dp, n_exp, across, queries, real_cols, granule, units = dims
    chips = n_dp // 2
    half = chips // 2
    slots, width = rows.shape
    model = width - units
    n_tok = by_token.shape[0]
    cols = fac.shape[1]
    me_e = lax.axis_index("expert")
    me = lax.axis_index("dp")
    core = me % 2
    other = 1 - core

    def walk(index):
        line, at = index // across, index % across
        back = line % 2
        return line * across + at + back * (across - 1 - 2 * at)

    place = walk(me // 2)

    def chip_at(step):
        return walk((place + step + chips) % chips)

    mine = chip_at(0)
    ahead = chip_at(1) * 2 + core
    behind = chip_at(-1) * 2 + core
    partner = mine * 2 + other

    pieces, start = [pl.ds(0, units)], units
    for part in V_EIGHTHS:
        pieces.append(pl.ds(start, part * model // 8))
        start += part * model // 8
    n_pieces = len(pieces)
    last_piece = n_pieces - 1

    def own(j):
        if j == 0:
            return gfac_hbm
        return vfac_hbm.at[:, pl.ds(pieces[j].start - units, pieces[j].size)]

    sent = []

    def send(src, dst, sem, target):
        copy = pltpu.make_async_remote_copy(
            src_ref=src,
            dst_ref=dst,
            send_sem=send_sem.at[0],
            recv_sem=sem,
            device_id=(me_e, target),
            device_id_type=MESH,
        )
        copy.start()
        sent.append(src.shape[0] * src.shape[1])

    def wait_for(ref, sem):
        pltpu.make_async_remote_copy(
            src_ref=ref,
            dst_ref=ref,
            send_sem=send_sem.at[0],
            recv_sem=sem,
            device_id=(me_e, partner),
            device_id_type=MESH,
        ).wait_recv()

    barrier = pltpu.get_barrier_semaphore()
    for target in (ahead, behind, partner):
        pl.semaphore_signal(barrier, inc=1, device_id=(me_e, target), device_id_type=MESH)
    for i in range(1, n_exp):
        pl.semaphore_signal(
            barrier, inc=1, device_id=((me_e + i) % n_exp, me), device_id_type=MESH
        )

    g_span, v_span = pl.ds(0, units), pl.ds(units, model)
    own_slot = mine * 2 + core
    load_tokens = pltpu.make_async_copy(token_hbm, tokens, load_sem.at[0])
    load_tokens.start()
    pltpu.make_async_copy(grads_hbm, rows.at[:, g_span], load_sem.at[1]).start()
    pltpu.make_async_copy(acts_hbm, rows.at[:, v_span], load_sem.at[1]).start()
    pltpu.make_async_copy(gfac_hbm, fac.at[own_slot, :, g_span], load_sem.at[2]).start()
    pltpu.make_async_copy(vfac_hbm, fac.at[own_slot, :, v_span], load_sem.at[2]).start()
    with jax.named_scope("barrier"):
        pl.semaphore_wait(barrier, 3 + n_exp - 1)

    for j in range(n_pieces):
        for target in (ahead, behind):
            send(own(j), fac.at[own_slot, :, pieces[j]], direct_sem.at[0, j], target)
    send(gfac_hbm, fac.at[own_slot, :, g_span], own_sem.at[0], partner)
    send(vfac_hbm, fac.at[own_slot, :, v_span], own_sem.at[0], partner)

    with jax.named_scope("onehot"):
        load_tokens.wait()
        slot_ids = lax.broadcasted_iota(jnp.int32, (1, slots), 1)
        names = jnp.where(slot_ids < count_ref[0, 0], tokens[...], -1)
        token_ids = lax.broadcasted_iota(jnp.int32, onehot.shape, 0)
        onehot[...] = (token_ids == names).astype(jnp.float32).astype(onehot.dtype)
        scores[...] = jnp.zeros_like(scores)
        far_dense[...] = jnp.zeros_like(far_dense)
        energies[...] = jnp.zeros_like(energies)

    with jax.named_scope("loadwait"):
        pltpu.make_async_copy(rows, rows, load_sem.at[1]).wait()

    def order_rows(first, size):
        part = jnp.dot(
            onehot[...], rows[:, first : first + size], preferred_element_type=jnp.float32
        )
        by_token[:, first : first + size] = part.astype(by_token.dtype)
        kind = int(first >= units)
        squares = part * part
        for i in range(size // LANES):
            energies[kind] += squares[:, i * LANES : (i + 1) * LANES]

    chunks = [(i, CHUNK) for i in range(0, width, CHUNK)]

    def project(factor, ref, span):
        return lax.dot_general(
            factor, ref[:, span], CONTRACT_LAST, preferred_element_type=jnp.float32
        )

    def project_pair(sources, span):
        factor = [fac[pl.ds(2 * chip, 2), :, span] for chip in sources]
        factor = jnp.concatenate([f.reshape(2 * cols, span.size) for f in factor], axis=0)
        return project(factor, by_token, span).reshape(len(sources), 2, cols, n_tok)

    def group_sums(chip, side, product):
        for i in range(real_cols // granule):
            query = ((2 * chip + side) * real_cols + i * granule) // RANK
            part = product[i * granule : (i + 1) * granule]
            yield query, jnp.sum(part, axis=0, keepdims=True)

    def owner_at(k):
        low = k + (k >= me_e).astype(jnp.int32)
        high = n_exp - 1 - k
        high = high - (high <= me_e).astype(jnp.int32)
        return jnp.where(2 * me_e < n_exp, high, low)

    def of_owner(owner):
        return pl.ds(pl.multiple_of(owner * TOK_DEV, TOK_DEV), TOK_DEV)

    def hand_over(stage, src, dst, owner, target=me):
        pltpu.make_async_remote_copy(
            src_ref=src,
            dst_ref=dst,
            send_sem=zsend_sem.at[stage],
            recv_sem=zrecv_sem.at[stage],
            device_id=(owner, target),
            device_id_type=MESH,
        ).start()

    def handed(stage, all_of):
        return pltpu.make_async_remote_copy(
            src_ref=all_of,
            dst_ref=all_of,
            send_sem=zsend_sem.at[stage],
            recv_sem=zrecv_sem.at[stage],
            device_id=((me_e + 1) % n_exp, me),
            device_id_type=MESH,
        )

    def sources_of(step):
        return [chip_at(-step)] if step == half else [chip_at(-step), chip_at(step)]

    def pass_on(step, j):
        sources = sources_of(step)
        count = len(sources)
        span = pieces[j]
        wait_for(fac.at[pl.ds(0, count), :, span], direct_sem.at[step - 1, j])

        def relay(chip, sem, target):
            part = fac.at[2 * chip + core, :, span]
            send(part, part, sem, target)

        if step < half - 1:
            relay(sources[0], direct_sem.at[step, j], ahead)
            relay(sources[1], direct_sem.at[step, j], behind)
        elif step == half - 1:
            chip = chip_at(step * (2 * core - 1))
            target = chip_at(1 - 2 * core) * 2 + core
            relay(chip, direct_sem.at[step, j], target)
        for chip in sources:
            relay(chip, relay_sem.at[step - 1, j], partner)

    def relayed(step, j):
        count = len(sources_of(step))
        wait_for(fac.at[pl.ds(0, count), :, pieces[j]], relay_sem.at[step - 1, j])

    far_chip = chip_at(half)

    def base_of(side):
        return (2 * far_chip + side) * real_cols // RANK

    def multiply(step, j):
        sources = sources_of(step)
        count = len(sources)
        relayed(step, j)
        value = project_pair(sources, pieces[j])
        if j == 0:
            gproj[:count] = value
        elif j == 1:
            aproj[:count] = value
        elif j < last_piece:
            aproj[:count] += value
        else:
            product = (aproj[:count] + value) * gproj[:count]
            for buf, chip in enumerate(sources):
                for side in range(2):
                    for query, total in group_sums(chip, side, product[buf, side]):
                        scores[pl.ds(query, 1)] += total

    far_owner = owner_at(0)
    edge_tok = of_owner(far_owner)
    rest = pl.ds(
        pl.multiple_of(jnp.where(far_owner == 0, TOK_DEV, 0), TOK_DEV), n_tok - TOK_DEV
    )

    def lend(part, span):
        pltpu.make_async_remote_copy(
            src_ref=by_token.at[edge_tok, span],
            dst_ref=mate.at[:, span],
            send_sem=mate_sem.at[2],
            recv_sem=mate_sem.at[part],
            device_id=(me_e, partner),
            device_id_type=MESH,
        ).start()

    with jax.named_scope("perm"):
        for at, chunk in enumerate(chunks):
            order_rows(*chunk)
            if chunk[0] == units:
                lend(0, g_span)
            if at == CHUNKS_BEFORE_RELAY - 1:
                with jax.named_scope("pass10"):
                    pass_on(1, 0)
    with jax.named_scope("energy"):
        totals = [
            jnp.sum(energies[kind].T, axis=0, keepdims=True) for kind in range(2)
        ]
        scores[queries : queries + 1] = totals[0] * totals[1]
    lend(1, v_span)

    with jax.named_scope("mineg"):
        own_shard = fac.at[own_slot]
        pltpu.make_async_copy(own_shard, own_shard, load_sem.at[2]).wait()
        wait_for(own_shard, own_sem.at[0])
        gproj[0] = project_pair([mine], g_span)[0]
    with jax.named_scope("pass11"):
        pass_on(1, 1)
    with jax.named_scope("minev"):
        product = project_pair([mine], v_span)[0] * gproj[0]
        for side in range(2):
            for query, total in group_sums(mine, side, product[side]):
                scores[pl.ds(query, 1)] += total

    def edge_products(j):
        factor = fac[2 * far_chip + core, :, pieces[j]]
        return [
            project(factor, by_token.at[edge_tok], pieces[j]),
            project(factor, mate, pieces[j]),
        ]

    def edge_multiply(j):
        if j < 2:
            wait_for(mate.at[:, (g_span, v_span)[j]], mate_sem.at[j])
        for kind, value in enumerate(edge_products(j)):
            if j == 0:
                edge_g[kind] = value
            elif j == 1:
                edge_a[kind] = value
            else:
                edge_a[kind] += value

    def rest_multiply(j):
        relayed(half, j)
        factor = fac[pl.ds(2 * far_chip, 2), :, pieces[j]]
        factor = factor.reshape(2 * cols, pieces[j].size)
        value = project(factor, by_token.at[rest], pieces[j])
        value = value.reshape(2, cols, n_tok - TOK_DEV)
        if j == 0:
            gproj[0, :, :, rest] = value
        elif j == 1:
            aproj[0, :, :, rest] = value
        else:
            aproj[0, :, :, rest] += value

    order = [(step, j) for step in range(1, half) for j in range(n_pieces)]
    for at, event in enumerate(order):
        if at > 1:
            with jax.named_scope(f"pass{event[0]}{event[1]}"):
                pass_on(*event)
        if at:
            with jax.named_scope(f"mul{order[at - 1][0]}{order[at - 1][1]}"):
                multiply(*order[at - 1])
    with jax.named_scope("mullast"):
        multiply(*order[-1])
    with jax.named_scope("near"):
        for k in range(n_exp - 1):
            owner = owner_at(k)
            hand_over(0, scores.at[:, of_owner(owner)], landed.at[me_e], owner)
    for j in range(last_piece):
        with jax.named_scope(f"pass{half}{j}"):
            pass_on(half, j)
        with jax.named_scope(f"edge{j}"):
            edge_multiply(j)
        if j:
            with jax.named_scope(f"rest{j - 1}"):
                rest_multiply(j - 1)
    with jax.named_scope(f"pass{half}{last_piece}"):
        pass_on(half, last_piece)

    def far_sums(owner, side, product):
        for query, total in group_sums(far_chip, side, product):
            far_dense[owner, side, query - base_of(side)] += total

    with jax.named_scope("edge"):
        for kind, value in enumerate(edge_products(last_piece)):
            product = (edge_a[kind] + value) * edge_g[kind]
            for query, total in group_sums(far_chip, core, product):
                far_dense[far_owner, kind, query - base_of(core)] += total
            hand_over(
                1,
                far_dense.at[far_owner, kind],
                far_landed.at[me_e, core],
                far_owner,
                partner if kind else me,
            )
    with jax.named_scope("restprev"):
        rest_multiply(last_piece - 1)
    with jax.named_scope("lastrelay"):
        relayed(half, last_piece)
    with jax.named_scope("far"):
        span = pieces[last_piece]
        factor = fac[pl.ds(2 * far_chip, 2), :, span].reshape(2 * cols, span.size)
        for k in range(1, n_exp):
            owner = owner_at(k) if k < n_exp - 1 else me_e
            tok = of_owner(owner)
            value = project(factor, by_token.at[tok], span).reshape(2, cols, TOK_DEV)
            for side in range(2):
                far_sums(
                    owner,
                    side,
                    (aproj[0, side, :, tok] + value[side]) * gproj[0, side, :, tok],
                )
            if k < n_exp - 1:
                hand_over(1, far_dense.at[owner], far_landed.at[me_e], owner)

    with jax.named_scope("colnear"):
        result = scores[:, of_owner(me_e)]
        near_wait = handed(0, landed.at[pl.ds(0, n_exp - 1)])
        near_wait.wait_recv()
        for k in range(n_exp - 1):
            result = result + landed[owner_at(k)]
        factor = lax.rsqrt(result[queries : queries + 1] / (model * units) + epsilon)
        factor = factor / jnp.sqrt(jnp.float32(RANK))
    with jax.named_scope("colfar"):
        far_wait = handed(1, far_landed.at[pl.ds(0, n_exp - 1)])
        far_wait.wait_recv()
    late = far_dense[me_e]
    for k in range(n_exp - 1):
        late = late + far_landed[owner_at(k)]
    row_ids = lax.broadcasted_iota(jnp.int32, result.shape, 0)
    for side in range(2):
        for i in range(late.shape[1]):
            row = row_ids == base_of(side) + i
            result = result + jnp.where(row, late[side, i], 0.0)
    out_ref[...] = result[:queries] * factor
    with jax.named_scope("sends"):
        near_wait.wait_send()
        far_wait.wait_send()

        def sent_all(ref, sem):
            pltpu.make_async_remote_copy(
                src_ref=ref,
                dst_ref=ref,
                send_sem=sem,
                recv_sem=own_sem.at[0],
                device_id=(me_e, partner),
                device_id_type=MESH,
            ).wait_send()

        sent_all(mate, mate_sem.at[2])
        sent_all(fac.at[pl.ds(0, sum(sent) // (cols * width))], send_sem.at[0])


def local(dims, row_acts, row_grads, grad_factor, value_factor, counts, row_token):
    n_dp, n_exp, across, queries, real_cols, granule = dims
    gfac, vfac = grad_factor[0].T, value_factor[0].T
    cols = round_up(real_cols, PACK)
    if cols != real_cols:
        pad = ((0, cols - real_cols), (0, 0))
        gfac, vfac = jnp.pad(gfac, pad), jnp.pad(vfac, pad)
    slots, model = row_acts.shape[1:]
    units = row_grads.shape[2]
    width = units + model
    chips = n_dp // 2
    steps = chips // 2
    depth = round_up(queries + 1, 8)
    n_tok = n_exp * TOK_DEV
    n_pieces = 1 + len(V_EIGHTHS)
    few = real_cols // RANK if real_cols % RANK == 0 else (real_cols - 1) // RANK + 2
    any_space = pl.BlockSpec(memory_space=pl.ANY)
    turned = pl.pallas_call(
        functools.partial(kernel, (*dims, units)),
        name="influence_exchange",
        out_shape=pltpu.VMEM((queries, TOK_DEV), jnp.float32),
        in_specs=[pl.BlockSpec(memory_space=pltpu.SMEM)] + [any_space] * 5,
        out_specs=pl.BlockSpec(memory_space=pltpu.VMEM),
        scratch_shapes=[
            pltpu.VMEM((1, slots), jnp.int32),
            pltpu.VMEM((slots, width), jnp.bfloat16),
            pltpu.VMEM((n_tok, width), jnp.bfloat16),
            pltpu.VMEM((TOK_DEV, width), jnp.bfloat16),
            pltpu.VMEM((n_dp, cols, width), jnp.bfloat16),
            pltpu.VMEM((2, 2, cols, n_tok), jnp.float32),
            pltpu.VMEM((2, 2, cols, n_tok), jnp.float32),
            pltpu.VMEM((2, cols, TOK_DEV), jnp.float32),
            pltpu.VMEM((2, cols, TOK_DEV), jnp.float32),
            pltpu.VMEM((depth, n_tok), jnp.float32),
            pltpu.VMEM((n_tok, slots), jnp.bfloat16),
            pltpu.VMEM((2, n_tok, LANES), jnp.float32),
            pltpu.VMEM((n_exp, depth, TOK_DEV), jnp.float32),
            pltpu.VMEM((n_exp, 2, few, 1, TOK_DEV), jnp.float32),
            pltpu.VMEM((n_exp, 2, few, 1, TOK_DEV), jnp.float32),
            pltpu.SemaphoreType.DMA((3,)),
            pltpu.SemaphoreType.DMA((1,)),
            pltpu.SemaphoreType.DMA((1,)),
            pltpu.SemaphoreType.DMA((steps, n_pieces)),
            pltpu.SemaphoreType.DMA((steps, n_pieces)),
            pltpu.SemaphoreType.DMA((3,)),
            pltpu.SemaphoreType.DMA((2,)),
            pltpu.SemaphoreType.DMA((2,)),
        ],
        compiler_params=pltpu.CompilerParams(
            collective_id=0, has_side_effects=True, vmem_limit_bytes=60 * 1024 * 1024
        ),
    )(counts, row_token, row_acts[0], row_grads[0], gfac, vfac)
    return turned.T


def solution(mesh):
    n_exp, n_dp = mesh.shape["expert"], mesh.shape["dp"]
    across = len({d.coords[0] for d in mesh.devices.flat})

    def whole(row_acts, row_grads, grad_factor, value_factor, counts, row_token):
        all_cols = grad_factor.shape[2]
        real_cols = all_cols // n_dp
        granule = real_cols if RANK % real_cols == 0 else RANK
        while real_cols % granule:
            granule //= 2
        dims = (n_dp, n_exp, across, all_cols // RANK, real_cols, granule)
        return jax.shard_map(
            functools.partial(local, dims),
            mesh=mesh,
            in_specs=(
                P("expert", "dp", None),
                P("expert", "dp", None),
                P("expert", None, "dp"),
                P("expert", None, "dp"),
                P("expert", "dp"),
                P("expert", "dp"),
            ),
            out_specs=P(("expert", "dp"), None),
            check_vma=False,
        )(row_acts, row_grads, grad_factor, value_factor, counts, row_token)

    return whole
```

```python
import functools

import jax
import jax.numpy as jnp
from jax import lax
from jax.experimental import pallas as pl
from jax.experimental.pallas import tpu as pltpu
from jax.sharding import PartitionSpec as P

RANK = 32
TOK_DEV = 256
LANES = 128
PACK = 16
V_EIGHTHS = (3, 2, 2, 1)
CHUNK = 256
CHUNKS_BEFORE_RELAY = 8

epsilon = 1e-06
MESH = pl.DeviceIdType.MESH
CONTRACT_LAST = (((1,), (1,)), ((), ()))


def round_up(value, unit):
    return -(-value // unit) * unit


def kernel(
    dims,
    count_ref,
    token_hbm,
    acts_hbm,
    grads_hbm,
    gfac_hbm,
    vfac_hbm,
    out_ref,
    tokens,
    rows,
    by_token,
    mate,
    fac,
    gproj,
    aproj,
    edge_g,
    edge_a,
    scores,
    onehot,
    energies,
    landed,
    far_dense,
    far_landed,
    load_sem,
    send_sem,
    own_sem,
    direct_sem,
    relay_sem,
    mate_sem,
    zsend_sem,
    zrecv_sem,
):
    n_dp, n_exp, across, queries, real_cols, granule, units = dims
    chips = n_dp // 2
    half = chips // 2
    slots, width = rows.shape
    model = width - units
    n_tok = by_token.shape[0]
    cols = fac.shape[1]
    me_e = lax.axis_index("expert")
    me = lax.axis_index("dp")
    core = me % 2
    other = 1 - core

    def walk(index):
        line, at = index // across, index % across
        back = line % 2
        return line * across + at + back * (across - 1 - 2 * at)

    place = walk(me // 2)

    def chip_at(step):
        return walk((place + step + chips) % chips)

    mine = chip_at(0)
    ahead = chip_at(1) * 2 + core
    behind = chip_at(-1) * 2 + core
    partner = mine * 2 + other

    pieces, start = [pl.ds(0, units)], units
    for part in V_EIGHTHS:
        pieces.append(pl.ds(start, part * model // 8))
        start += part * model // 8
    n_pieces = len(pieces)
    last_piece = n_pieces - 1

    def own(j):
        if j == 0:
            return gfac_hbm
        return vfac_hbm.at[:, pl.ds(pieces[j].start - units, pieces[j].size)]

    sent = []

    def send(src, dst, sem, target):
        copy = pltpu.make_async_remote_copy(
            src_ref=src,
            dst_ref=dst,
            send_sem=send_sem.at[0],
            recv_sem=sem,
            device_id=(me_e, target),
            device_id_type=MESH,
        )
        copy.start()
        sent.append(src.shape[0] * src.shape[1])

    def wait_for(ref, sem):
        pltpu.make_async_remote_copy(
            src_ref=ref,
            dst_ref=ref,
            send_sem=send_sem.at[0],
            recv_sem=sem,
            device_id=(me_e, partner),
            device_id_type=MESH,
        ).wait_recv()

    barrier = pltpu.get_barrier_semaphore()
    for target in (ahead, behind, partner):
        pl.semaphore_signal(barrier, inc=1, device_id=(me_e, target), device_id_type=MESH)
    for i in range(1, n_exp):
        pl.semaphore_signal(
            barrier, inc=1, device_id=((me_e + i) % n_exp, me), device_id_type=MESH
        )

    g_span, v_span = pl.ds(0, units), pl.ds(units, model)
    own_slot = mine * 2 + core
    load_tokens = pltpu.make_async_copy(token_hbm, tokens, load_sem.at[0])
    load_tokens.start()
    pltpu.make_async_copy(grads_hbm, rows.at[:, g_span], load_sem.at[1]).start()
    pltpu.make_async_copy(acts_hbm, rows.at[:, v_span], load_sem.at[1]).start()
    pltpu.make_async_copy(gfac_hbm, fac.at[own_slot, :, g_span], load_sem.at[2]).start()
    pltpu.make_async_copy(vfac_hbm, fac.at[own_slot, :, v_span], load_sem.at[2]).start()
    with jax.named_scope("barrier"):
        pl.semaphore_wait(barrier, 3 + n_exp - 1)

    for j in range(n_pieces):
        for target in (ahead, behind):
            send(own(j), fac.at[own_slot, :, pieces[j]], direct_sem.at[0, j], target)
    send(gfac_hbm, fac.at[own_slot, :, g_span], own_sem.at[0], partner)
    send(vfac_hbm, fac.at[own_slot, :, v_span], own_sem.at[0], partner)

    with jax.named_scope("onehot"):
        load_tokens.wait()
        slot_ids = lax.broadcasted_iota(jnp.int32, (1, slots), 1)
        names = jnp.where(slot_ids < count_ref[0, 0], tokens[...], -1)
        token_ids = lax.broadcasted_iota(jnp.int32, onehot.shape, 0)
        onehot[...] = (token_ids == names).astype(jnp.float32).astype(onehot.dtype)
        scores[...] = jnp.zeros_like(scores)
        far_dense[...] = jnp.zeros_like(far_dense)
        energies[...] = jnp.zeros_like(energies)

    with jax.named_scope("loadwait"):
        pltpu.make_async_copy(rows, rows, load_sem.at[1]).wait()

    def order_rows(first, size):
        part = jnp.dot(
            onehot[...], rows[:, first : first + size], preferred_element_type=jnp.float32
        )
        by_token[:, first : first + size] = part.astype(by_token.dtype)
        kind = int(first >= units)
        squares = part * part
        for i in range(size // LANES):
            energies[kind] += squares[:, i * LANES : (i + 1) * LANES]

    chunks = [(i, CHUNK) for i in range(0, width, CHUNK)]

    def project(factor, ref, span):
        return lax.dot_general(
            factor, ref[:, span], CONTRACT_LAST, preferred_element_type=jnp.float32
        )

    def project_pair(sources, span):
        factor = [fac[pl.ds(2 * chip, 2), :, span] for chip in sources]
        factor = jnp.concatenate([f.reshape(2 * cols, span.size) for f in factor], axis=0)
        return project(factor, by_token, span).reshape(len(sources), 2, cols, n_tok)

    def group_sums(chip, side, product):
        for i in range(real_cols // granule):
            query = ((2 * chip + side) * real_cols + i * granule) // RANK
            part = product[i * granule : (i + 1) * granule]
            yield query, jnp.sum(part, axis=0, keepdims=True)

    def owner_at(k):
        low = k + (k >= me_e).astype(jnp.int32)
        high = n_exp - 1 - k
        high = high - (high <= me_e).astype(jnp.int32)
        return jnp.where(2 * me_e < n_exp, high, low)

    def of_owner(owner):
        return pl.ds(pl.multiple_of(owner * TOK_DEV, TOK_DEV), TOK_DEV)

    def hand_over(stage, src, dst, owner, target=me):
        pltpu.make_async_remote_copy(
            src_ref=src,
            dst_ref=dst,
            send_sem=zsend_sem.at[stage],
            recv_sem=zrecv_sem.at[stage],
            device_id=(owner, target),
            device_id_type=MESH,
        ).start()

    def handed(stage, all_of):
        return pltpu.make_async_remote_copy(
            src_ref=all_of,
            dst_ref=all_of,
            send_sem=zsend_sem.at[stage],
            recv_sem=zrecv_sem.at[stage],
            device_id=((me_e + 1) % n_exp, me),
            device_id_type=MESH,
        )

    def sources_of(step):
        return [chip_at(-step)] if step == half else [chip_at(-step), chip_at(step)]

    def pass_on(step, j):
        sources = sources_of(step)
        count = len(sources)
        span = pieces[j]
        wait_for(fac.at[pl.ds(0, count), :, span], direct_sem.at[step - 1, j])

        def relay(chip, sem, target):
            part = fac.at[2 * chip + core, :, span]
            send(part, part, sem, target)

        if step < half - 1:
            relay(sources[0], direct_sem.at[step, j], ahead)
            relay(sources[1], direct_sem.at[step, j], behind)
        elif step == half - 1:
            chip = chip_at(step * (2 * core - 1))
            target = chip_at(1 - 2 * core) * 2 + core
            relay(chip, direct_sem.at[step, j], target)
        for chip in sources:
            relay(chip, relay_sem.at[step - 1, j], partner)

    def relayed(step, j):
        count = len(sources_of(step))
        wait_for(fac.at[pl.ds(0, count), :, pieces[j]], relay_sem.at[step - 1, j])

    far_chip = chip_at(half)

    def base_of(side):
        return (2 * far_chip + side) * real_cols // RANK

    def multiply(step, j):
        sources = sources_of(step)
        count = len(sources)
        relayed(step, j)
        value = project_pair(sources, pieces[j])
        if j == 0:
            gproj[:count] = value
        elif j == 1:
            aproj[:count] = value
        elif j < last_piece:
            aproj[:count] += value
        else:
            product = (aproj[:count] + value) * gproj[:count]
            for buf, chip in enumerate(sources):
                for side in range(2):
                    for query, total in group_sums(chip, side, product[buf, side]):
                        scores[pl.ds(query, 1)] += total

    edge = mate.shape[0]
    lower = 2 * me_e < n_exp
    edge_start = pl.multiple_of(jnp.where(lower, n_tok - edge, 0), TOK_DEV)
    rest_start = pl.multiple_of(jnp.where(lower, 0, edge), TOK_DEV)
    edge_tok, rest = pl.ds(edge_start, edge), pl.ds(rest_start, n_tok - edge)
    middle = pieces[3].start
    mate_spans = [
        g_span, pl.ds(units, middle - units), pl.ds(middle, width - middle)
    ]

    def lend(part):
        span = mate_spans[part]
        pltpu.make_async_remote_copy(
            src_ref=by_token.at[edge_tok, span],
            dst_ref=mate.at[:, span],
            send_sem=mate_sem.at[3],
            recv_sem=mate_sem.at[part],
            device_id=(me_e, partner),
            device_id_type=MESH,
        ).start()

    with jax.named_scope("perm"):
        for at, chunk in enumerate(chunks):
            order_rows(*chunk)
            for part in range(2):
                if chunk[0] == mate_spans[part + 1].start:
                    lend(part)
            if at == CHUNKS_BEFORE_RELAY - 1:
                with jax.named_scope("pass10"):
                    pass_on(1, 0)
    with jax.named_scope("energy"):
        totals = [
            jnp.sum(energies[kind].T, axis=0, keepdims=True) for kind in range(2)
        ]
        scores[queries : queries + 1] = totals[0] * totals[1]
    lend(2)

    with jax.named_scope("mineg"):
        own_shard = fac.at[own_slot]
        pltpu.make_async_copy(own_shard, own_shard, load_sem.at[2]).wait()
        wait_for(own_shard, own_sem.at[0])
        gproj[0] = project_pair([mine], g_span)[0]
    with jax.named_scope("pass11"):
        pass_on(1, 1)
    with jax.named_scope("minev"):
        product = project_pair([mine], v_span)[0] * gproj[0]
        for side in range(2):
            for query, total in group_sums(mine, side, product[side]):
                scores[pl.ds(query, 1)] += total

    def edge_product(j):
        for part, span in enumerate(mate_spans):
            if pieces[j].start == span.start:
                wait_for(mate.at[:, span], mate_sem.at[part])
        factor = fac[2 * far_chip + core, :, pieces[j]]
        both = jnp.concatenate([by_token[edge_tok, pieces[j]], mate[:, pieces[j]]], axis=0)
        value = lax.dot_general(
            factor, both, CONTRACT_LAST, preferred_element_type=jnp.float32
        )
        return [value[:, :edge], value[:, edge:]]

    def edge_multiply(j):
        for kind, part in enumerate(edge_product(j)):
            if j == 0:
                edge_g[kind] = part
            elif j == 1:
                edge_a[kind] = part
            else:
                edge_a[kind] += part

    def rest_product(j):
        factor = fac[pl.ds(2 * far_chip, 2), :, pieces[j]]
        factor = factor.reshape(2 * cols, pieces[j].size)
        value = project(factor, by_token.at[rest], pieces[j])
        return value.reshape(2, cols, n_tok - edge)

    def rest_multiply(j):
        relayed(half, j)
        value = rest_product(j)
        if j == 0:
            gproj[0, :, :, rest] = value
        elif j == 1:
            aproj[0, :, :, rest] = value
        else:
            aproj[0, :, :, rest] += value

    order = [(step, j) for step in range(1, half) for j in range(n_pieces)]
    for at, event in enumerate(order):
        if at > 1:
            with jax.named_scope(f"pass{event[0]}{event[1]}"):
                pass_on(*event)
        if at:
            with jax.named_scope(f"mul{order[at - 1][0]}{order[at - 1][1]}"):
                multiply(*order[at - 1])
    with jax.named_scope("mullast"):
        multiply(*order[-1])
    with jax.named_scope("near"):
        for k in range(n_exp - 1):
            owner = owner_at(k)
            hand_over(0, scores.at[:, of_owner(owner)], landed.at[me_e], owner)
    for j in range(last_piece):
        with jax.named_scope(f"pass{half}{j}"):
            pass_on(half, j)
        with jax.named_scope(f"edge{j}"):
            edge_multiply(j)
        if j > 1:
            with jax.named_scope(f"rest{j - 2}"):
                rest_multiply(j - 2)
    with jax.named_scope(f"pass{half}{last_piece}"):
        pass_on(half, last_piece)

    def far_sums(kind, side, product, first, count):
        for query, total in group_sums(far_chip, side, product):
            for i in range(count):
                far_dense[first + i, kind, query - base_of(side)] += total[
                    :, i * TOK_DEV : (i + 1) * TOK_DEV
                ]

    n_edge = edge // TOK_DEV
    edge_first = jnp.where(lower, n_exp - n_edge, 0)
    rest_first = jnp.where(lower, 0, n_edge)
    with jax.named_scope("edge"):
        for kind, value in enumerate(edge_product(last_piece)):
            product = (edge_a[kind] + value) * edge_g[kind]
            far_sums(kind, core, product, edge_first, n_edge)
            for k in range(n_edge):
                hand_over(
                    1,
                    far_dense.at[owner_at(k), kind],
                    far_landed.at[me_e, core],
                    owner_at(k),
                    partner if kind else me,
                )
    for j in range(max(last_piece - 2, 0), last_piece):
        with jax.named_scope(f"rest{j}"):
            rest_multiply(j)
    with jax.named_scope("lastrelay"):
        relayed(half, last_piece)
    with jax.named_scope("far"):
        value = rest_product(last_piece)
        for side in range(2):
            product = (aproj[0, side, :, rest] + value[side]) * gproj[0, side, :, rest]
            far_sums(side, side, product, rest_first, n_exp - n_edge)
        for k in range(n_edge, n_exp - 1):
            owner = owner_at(k)
            hand_over(1, far_dense.at[owner], far_landed.at[me_e], owner)

    with jax.named_scope("colnear"):
        result = scores[:, of_owner(me_e)]
        near_wait = handed(0, landed.at[pl.ds(0, n_exp - 1)])
        near_wait.wait_recv()
        for k in range(n_exp - 1):
            result = result + landed[owner_at(k)]
        factor = lax.rsqrt(result[queries : queries + 1] / (model * units) + epsilon)
        factor = factor / jnp.sqrt(jnp.float32(RANK))
    with jax.named_scope("colfar"):
        far_wait = handed(1, far_landed.at[pl.ds(0, n_exp - 1)])
        far_wait.wait_recv()
    late = far_dense[me_e]
    for k in range(n_exp - 1):
        late = late + far_landed[owner_at(k)]
    row_ids = lax.broadcasted_iota(jnp.int32, result.shape, 0)
    for side in range(2):
        for i in range(late.shape[1]):
            row = row_ids == base_of(side) + i
            result = result + jnp.where(row, late[side, i], 0.0)
    out_ref[...] = result[:queries] * factor
    with jax.named_scope("sends"):
        near_wait.wait_send()
        far_wait.wait_send()

        def sent_all(ref, sem):
            pltpu.make_async_remote_copy(
                src_ref=ref,
                dst_ref=ref,
                send_sem=sem,
                recv_sem=own_sem.at[0],
                device_id=(me_e, partner),
                device_id_type=MESH,
            ).wait_send()

        sent_all(mate, mate_sem.at[3])
        sent_all(fac.at[pl.ds(0, sum(sent) // (cols * width))], send_sem.at[0])


def local(dims, row_acts, row_grads, grad_factor, value_factor, counts, row_token):
    n_dp, n_exp, across, queries, real_cols, granule = dims
    gfac, vfac = grad_factor[0].T, value_factor[0].T
    cols = round_up(real_cols, PACK)
    if cols != real_cols:
        pad = ((0, cols - real_cols), (0, 0))
        gfac, vfac = jnp.pad(gfac, pad), jnp.pad(vfac, pad)
    slots, model = row_acts.shape[1:]
    units = row_grads.shape[2]
    width = units + model
    chips = n_dp // 2
    steps = chips // 2
    depth = round_up(queries + 1, 8)
    n_tok = n_exp * TOK_DEV
    edge = n_exp // 2 * TOK_DEV
    n_pieces = 1 + len(V_EIGHTHS)
    few = real_cols // RANK if real_cols % RANK == 0 else (real_cols - 1) // RANK + 2
    any_space = pl.BlockSpec(memory_space=pl.ANY)
    turned = pl.pallas_call(
        functools.partial(kernel, (*dims, units)),
        name="influence_exchange",
        out_shape=pltpu.VMEM((queries, TOK_DEV), jnp.float32),
        in_specs=[pl.BlockSpec(memory_space=pltpu.SMEM)] + [any_space] * 5,
        out_specs=pl.BlockSpec(memory_space=pltpu.VMEM),
        scratch_shapes=[
            pltpu.VMEM((1, slots), jnp.int32),
            pltpu.VMEM((slots, width), jnp.bfloat16),
            pltpu.VMEM((n_tok, width), jnp.bfloat16),
            pltpu.VMEM((edge, width), jnp.bfloat16),
            pltpu.VMEM((n_dp, cols, width), jnp.bfloat16),
            pltpu.VMEM((2, 2, cols, n_tok), jnp.float32),
            pltpu.VMEM((2, 2, cols, n_tok), jnp.float32),
            pltpu.VMEM((2, cols, edge), jnp.float32),
            pltpu.VMEM((2, cols, edge), jnp.float32),
            pltpu.VMEM((depth, n_tok), jnp.float32),
            pltpu.VMEM((n_tok, slots), jnp.bfloat16),
            pltpu.VMEM((2, n_tok, LANES), jnp.float32),
            pltpu.VMEM((n_exp, depth, TOK_DEV), jnp.float32),
            pltpu.VMEM((n_exp, 2, few, 1, TOK_DEV), jnp.float32),
            pltpu.VMEM((n_exp, 2, few, 1, TOK_DEV), jnp.float32),
            pltpu.SemaphoreType.DMA((3,)),
            pltpu.SemaphoreType.DMA((1,)),
            pltpu.SemaphoreType.DMA((1,)),
            pltpu.SemaphoreType.DMA((steps, n_pieces)),
            pltpu.SemaphoreType.DMA((steps, n_pieces)),
            pltpu.SemaphoreType.DMA((4,)),
            pltpu.SemaphoreType.DMA((2,)),
            pltpu.SemaphoreType.DMA((2,)),
        ],
        compiler_params=pltpu.CompilerParams(
            collective_id=0, has_side_effects=True, vmem_limit_bytes=60 * 1024 * 1024
        ),
    )(counts, row_token, row_acts[0], row_grads[0], gfac, vfac)
    return turned.T


def solution(mesh):
    n_exp, n_dp = mesh.shape["expert"], mesh.shape["dp"]
    across = len({d.coords[0] for d in mesh.devices.flat})

    def whole(row_acts, row_grads, grad_factor, value_factor, counts, row_token):
        all_cols = grad_factor.shape[2]
        real_cols = all_cols // n_dp
        granule = real_cols if RANK % real_cols == 0 else RANK
        while real_cols % granule:
            granule //= 2
        dims = (n_dp, n_exp, across, all_cols // RANK, real_cols, granule)
        return jax.shard_map(
            functools.partial(local, dims),
            mesh=mesh,
            in_specs=(
                P("expert", "dp", None),
                P("expert", "dp", None),
                P("expert", None, "dp"),
                P("expert", None, "dp"),
                P("expert", "dp"),
                P("expert", "dp"),
            ),
            out_specs=P(("expert", "dp"), None),
            check_vma=False,
        )(row_acts, row_grads, grad_factor, value_factor, counts, row_token)

    return whole
```

```python
import functools

import jax
import jax.numpy as jnp
from jax import lax
from jax.experimental import pallas as pl
from jax.experimental.pallas import tpu as pltpu
from jax.sharding import PartitionSpec as P

RANK = 32
TOK_DEV = 256
LANES = 128
PACK = 16
V_EIGHTHS = (3, 2, 2, 1)
CHUNK = 256
CHUNKS_BEFORE_RELAY = 8

epsilon = 1e-06
MESH = pl.DeviceIdType.MESH
CONTRACT_LAST = (((1,), (1,)), ((), ()))


def round_up(value, unit):
    return -(-value // unit) * unit


def kernel(
    dims,
    count_ref,
    token_hbm,
    acts_hbm,
    grads_hbm,
    gfac_hbm,
    vfac_hbm,
    out_ref,
    tokens,
    rows,
    by_token,
    mate,
    fac,
    gproj,
    aproj,
    edge_g,
    edge_a,
    scores,
    onehot,
    energies,
    landed,
    far_dense,
    far_landed,
    load_sem,
    send_sem,
    own_sem,
    direct_sem,
    relay_sem,
    mate_sem,
    zsend_sem,
    zrecv_sem,
):
    n_dp, n_exp, across, queries, real_cols, granule, units = dims
    chips = n_dp // 2
    half = chips // 2
    slots, width = rows.shape
    model = width - units
    n_tok = by_token.shape[0]
    cols = fac.shape[1]
    me_e = lax.axis_index("expert")
    me = lax.axis_index("dp")
    core = me % 2
    other = 1 - core

    def walk(index):
        line, at = index // across, index % across
        back = line % 2
        return line * across + at + back * (across - 1 - 2 * at)

    place = walk(me // 2)

    def chip_at(step):
        return walk((place + step + chips) % chips)

    mine = chip_at(0)
    ahead = chip_at(1) * 2 + core
    behind = chip_at(-1) * 2 + core
    partner = mine * 2 + other

    pieces, start = [pl.ds(0, units)], units
    for part in V_EIGHTHS:
        pieces.append(pl.ds(start, part * model // 8))
        start += part * model // 8
    n_pieces = len(pieces)
    last_piece = n_pieces - 1

    def own(j):
        if j == 0:
            return gfac_hbm
        return vfac_hbm.at[:, pl.ds(pieces[j].start - units, pieces[j].size)]

    sent = []

    def send(src, dst, sem, target):
        copy = pltpu.make_async_remote_copy(
            src_ref=src,
            dst_ref=dst,
            send_sem=send_sem.at[0],
            recv_sem=sem,
            device_id=(me_e, target),
            device_id_type=MESH,
        )
        copy.start()
        sent.append(src.shape[0] * src.shape[1])

    def wait_for(ref, sem):
        pltpu.make_async_remote_copy(
            src_ref=ref,
            dst_ref=ref,
            send_sem=send_sem.at[0],
            recv_sem=sem,
            device_id=(me_e, partner),
            device_id_type=MESH,
        ).wait_recv()

    barrier = pltpu.get_barrier_semaphore()
    for target in (ahead, behind, partner):
        pl.semaphore_signal(barrier, inc=1, device_id=(me_e, target), device_id_type=MESH)
    for i in range(1, n_exp):
        pl.semaphore_signal(
            barrier, inc=1, device_id=((me_e + i) % n_exp, me), device_id_type=MESH
        )

    g_span, v_span = pl.ds(0, units), pl.ds(units, model)
    own_slot = mine * 2 + core
    load_tokens = pltpu.make_async_copy(token_hbm, tokens, load_sem.at[0])
    load_tokens.start()
    pltpu.make_async_copy(gfac_hbm, fac.at[own_slot, :, g_span], load_sem.at[2]).start()
    pltpu.make_async_copy(vfac_hbm, fac.at[own_slot, :, v_span], load_sem.at[2]).start()
    pltpu.make_async_copy(grads_hbm, rows.at[:, g_span], load_sem.at[1]).start()
    pltpu.make_async_copy(acts_hbm, rows.at[:, v_span], load_sem.at[1]).start()
    with jax.named_scope("barrier"):
        pl.semaphore_wait(barrier, 3 + n_exp - 1)

    own_shard = fac.at[own_slot]
    pltpu.make_async_copy(own_shard, own_shard, load_sem.at[2]).wait()
    for j in range(n_pieces):
        for target in (ahead, behind):
            part = fac.at[own_slot, :, pieces[j]]
            send(part, part, direct_sem.at[0, j], target)
    send(own_shard, own_shard, own_sem.at[0], partner)

    with jax.named_scope("onehot"):
        load_tokens.wait()
        slot_ids = lax.broadcasted_iota(jnp.int32, (1, slots), 1)
        names = jnp.where(slot_ids < count_ref[0, 0], tokens[...], -1)
        token_ids = lax.broadcasted_iota(jnp.int32, onehot.shape, 0)
        onehot[...] = (token_ids == names).astype(jnp.float32).astype(onehot.dtype)
        scores[...] = jnp.zeros_like(scores)
        far_dense[...] = jnp.zeros_like(far_dense)
        energies[...] = jnp.zeros_like(energies)

    with jax.named_scope("loadwait"):
        pltpu.make_async_copy(rows, rows, load_sem.at[1]).wait()

    def order_rows(first, size):
        part = jnp.dot(
            onehot[...], rows[:, first : first + size], preferred_element_type=jnp.float32
        )
        by_token[:, first : first + size] = part.astype(by_token.dtype)
        kind = int(first >= units)
        squares = part * part
        for i in range(size // LANES):
            energies[kind] += squares[:, i * LANES : (i + 1) * LANES]

    chunks = [(i, CHUNK) for i in range(0, width, CHUNK)]

    def project(factor, ref, span):
        return lax.dot_general(
            factor, ref[:, span], CONTRACT_LAST, preferred_element_type=jnp.float32
        )

    def project_pair(sources, span):
        factor = [fac[pl.ds(2 * chip, 2), :, span] for chip in sources]
        factor = jnp.concatenate([f.reshape(2 * cols, span.size) for f in factor], axis=0)
        return project(factor, by_token, span).reshape(len(sources), 2, cols, n_tok)

    def group_sums(chip, side, product):
        for i in range(real_cols // granule):
            query = ((2 * chip + side) * real_cols + i * granule) // RANK
            part = product[i * granule : (i + 1) * granule]
            yield query, jnp.sum(part, axis=0, keepdims=True)

    def owner_at(k):
        low = k + (k >= me_e).astype(jnp.int32)
        high = n_exp - 1 - k
        high = high - (high <= me_e).astype(jnp.int32)
        return jnp.where(2 * me_e < n_exp, high, low)

    def of_owner(owner):
        return pl.ds(pl.multiple_of(owner * TOK_DEV, TOK_DEV), TOK_DEV)

    def hand_over(stage, src, dst, owner, target=me):
        pltpu.make_async_remote_copy(
            src_ref=src,
            dst_ref=dst,
            send_sem=zsend_sem.at[stage],
            recv_sem=zrecv_sem.at[stage],
            device_id=(owner, target),
            device_id_type=MESH,
        ).start()

    def handed(stage, all_of):
        return pltpu.make_async_remote_copy(
            src_ref=all_of,
            dst_ref=all_of,
            send_sem=zsend_sem.at[stage],
            recv_sem=zrecv_sem.at[stage],
            device_id=((me_e + 1) % n_exp, me),
            device_id_type=MESH,
        )

    def sources_of(step):
        return [chip_at(-step)] if step == half else [chip_at(-step), chip_at(step)]

    def pass_on(step, j):
        sources = sources_of(step)
        count = len(sources)
        span = pieces[j]
        wait_for(fac.at[pl.ds(0, count), :, span], direct_sem.at[step - 1, j])

        def relay(chip, sem, target):
            part = fac.at[2 * chip + core, :, span]
            send(part, part, sem, target)

        if step < half - 1:
            relay(sources[0], direct_sem.at[step, j], ahead)
            relay(sources[1], direct_sem.at[step, j], behind)
        elif step == half - 1:
            chip = chip_at(step * (2 * core - 1))
            target = chip_at(1 - 2 * core) * 2 + core
            relay(chip, direct_sem.at[step, j], target)
        for chip in sources:
            relay(chip, relay_sem.at[step - 1, j], partner)

    def relayed(step, j):
        count = len(sources_of(step))
        wait_for(fac.at[pl.ds(0, count), :, pieces[j]], relay_sem.at[step - 1, j])

    far_chip = chip_at(half)

    def base_of(side):
        return (2 * far_chip + side) * real_cols // RANK

    def multiply(step, j):
        sources = sources_of(step)
        count = len(sources)
        relayed(step, j)
        value = project_pair(sources, pieces[j])
        if j == 0:
            gproj[:count] = value
        elif j == 1:
            aproj[:count] = value
        elif j < last_piece:
            aproj[:count] += value
        else:
            product = (aproj[:count] + value) * gproj[:count]
            for buf, chip in enumerate(sources):
                for side in range(2):
                    for query, total in group_sums(chip, side, product[buf, side]):
                        scores[pl.ds(query, 1)] += total

    edge = mate.shape[0]
    lower = 2 * me_e < n_exp
    edge_start = pl.multiple_of(jnp.where(lower, n_tok - edge, 0), TOK_DEV)
    rest_start = pl.multiple_of(jnp.where(lower, 0, edge), TOK_DEV)
    edge_tok, rest = pl.ds(edge_start, edge), pl.ds(rest_start, n_tok - edge)
    middle = pieces[3].start
    mate_spans = [
        g_span, pl.ds(units, middle - units), pl.ds(middle, width - middle)
    ]

    def lend(part):
        span = mate_spans[part]
        pltpu.make_async_remote_copy(
            src_ref=by_token.at[edge_tok, span],
            dst_ref=mate.at[:, span],
            send_sem=mate_sem.at[3],
            recv_sem=mate_sem.at[part],
            device_id=(me_e, partner),
            device_id_type=MESH,
        ).start()

    with jax.named_scope("perm"):
        for at, chunk in enumerate(chunks):
            order_rows(*chunk)
            for part in range(2):
                if chunk[0] == mate_spans[part + 1].start:
                    lend(part)
            if at == CHUNKS_BEFORE_RELAY - 1:
                with jax.named_scope("pass10"):
                    pass_on(1, 0)
    with jax.named_scope("energy"):
        totals = [
            jnp.sum(energies[kind].T, axis=0, keepdims=True) for kind in range(2)
        ]
        scores[queries : queries + 1] = totals[0] * totals[1]
    lend(2)

    with jax.named_scope("mineg"):
        own_shard = fac.at[own_slot]
        wait_for(own_shard, own_sem.at[0])
        gproj[0] = project_pair([mine], g_span)[0]
    with jax.named_scope("pass11"):
        pass_on(1, 1)
    with jax.named_scope("minev"):
        product = project_pair([mine], v_span)[0] * gproj[0]
        for side in range(2):
            for query, total in group_sums(mine, side, product[side]):
                scores[pl.ds(query, 1)] += total

    def edge_product(j):
        for part, span in enumerate(mate_spans):
            if pieces[j].start == span.start:
                wait_for(mate.at[:, span], mate_sem.at[part])
        factor = fac[2 * far_chip + core, :, pieces[j]]
        both = jnp.concatenate([by_token[edge_tok, pieces[j]], mate[:, pieces[j]]], axis=0)
        value = lax.dot_general(
            factor, both, CONTRACT_LAST, preferred_element_type=jnp.float32
        )
        return [value[:, :edge], value[:, edge:]]

    def edge_multiply(j):
        for kind, part in enumerate(edge_product(j)):
            if j == 0:
                edge_g[kind] = part
            elif j == 1:
                edge_a[kind] = part
            else:
                edge_a[kind] += part

    def rest_product(j):
        factor = fac[pl.ds(2 * far_chip, 2), :, pieces[j]]
        factor = factor.reshape(2 * cols, pieces[j].size)
        value = project(factor, by_token.at[rest], pieces[j])
        return value.reshape(2, cols, n_tok - edge)

    def rest_multiply(j):
        relayed(half, j)
        value = rest_product(j)
        if j == 0:
            gproj[0, :, :, rest] = value
        elif j == 1:
            aproj[0, :, :, rest] = value
        else:
            aproj[0, :, :, rest] += value

    order = [(step, j) for step in range(1, half) for j in range(n_pieces)]
    for at, event in enumerate(order):
        if at > 1:
            with jax.named_scope(f"pass{event[0]}{event[1]}"):
                pass_on(*event)
        if at:
            with jax.named_scope(f"mul{order[at - 1][0]}{order[at - 1][1]}"):
                multiply(*order[at - 1])
    with jax.named_scope("mullast"):
        multiply(*order[-1])
    with jax.named_scope("near"):
        for k in range(n_exp - 1):
            owner = owner_at(k)
            hand_over(0, scores.at[:, of_owner(owner)], landed.at[me_e], owner)
    for j in range(last_piece):
        with jax.named_scope(f"pass{half}{j}"):
            pass_on(half, j)
        with jax.named_scope(f"edge{j}"):
            edge_multiply(j)
        if j > 1:
            with jax.named_scope(f"rest{j - 2}"):
                rest_multiply(j - 2)
    with jax.named_scope(f"pass{half}{last_piece}"):
        pass_on(half, last_piece)

    def far_sums(kind, side, product, first, count):
        for query, total in group_sums(far_chip, side, product):
            for i in range(count):
                far_dense[first + i, kind, query - base_of(side)] += total[
                    :, i * TOK_DEV : (i + 1) * TOK_DEV
                ]

    n_edge = edge // TOK_DEV
    edge_first = jnp.where(lower, n_exp - n_edge, 0)
    rest_first = jnp.where(lower, 0, n_edge)
    with jax.named_scope("edge"):
        for kind, value in enumerate(edge_product(last_piece)):
            product = (edge_a[kind] + value) * edge_g[kind]
            far_sums(kind, core, product, edge_first, n_edge)
            for k in range(n_edge):
                hand_over(
                    1,
                    far_dense.at[owner_at(k), kind],
                    far_landed.at[me_e, core],
                    owner_at(k),
                    partner if kind else me,
                )
    for j in range(max(last_piece - 2, 0), last_piece):
        with jax.named_scope(f"rest{j}"):
            rest_multiply(j)
    with jax.named_scope("lastrelay"):
        relayed(half, last_piece)
    with jax.named_scope("far"):
        value = rest_product(last_piece)
        for side in range(2):
            product = (aproj[0, side, :, rest] + value[side]) * gproj[0, side, :, rest]
            far_sums(side, side, product, rest_first, n_exp - n_edge)
        for k in range(n_edge, n_exp - 1):
            owner = owner_at(k)
            hand_over(1, far_dense.at[owner], far_landed.at[me_e], owner)

    with jax.named_scope("colnear"):
        result = scores[:, of_owner(me_e)]
        near_wait = handed(0, landed.at[pl.ds(0, n_exp - 1)])
        near_wait.wait_recv()
        for k in range(n_exp - 1):
            result = result + landed[owner_at(k)]
        factor = lax.rsqrt(result[queries : queries + 1] / (model * units) + epsilon)
        factor = factor / jnp.sqrt(jnp.float32(RANK))
    with jax.named_scope("colfar"):
        far_wait = handed(1, far_landed.at[pl.ds(0, n_exp - 1)])
        far_wait.wait_recv()
    late = far_dense[me_e]
    for k in range(n_exp - 1):
        late = late + far_landed[owner_at(k)]
    row_ids = lax.broadcasted_iota(jnp.int32, result.shape, 0)
    for side in range(2):
        for i in range(late.shape[1]):
            row = row_ids == base_of(side) + i
            result = result + jnp.where(row, late[side, i], 0.0)
    out_ref[...] = result[:queries] * factor
    with jax.named_scope("sends"):
        near_wait.wait_send()
        far_wait.wait_send()

        def sent_all(ref, sem):
            pltpu.make_async_remote_copy(
                src_ref=ref,
                dst_ref=ref,
                send_sem=sem,
                recv_sem=own_sem.at[0],
                device_id=(me_e, partner),
                device_id_type=MESH,
            ).wait_send()

        sent_all(mate, mate_sem.at[3])
        sent_all(fac.at[pl.ds(0, sum(sent) // (cols * width))], send_sem.at[0])


def local(dims, row_acts, row_grads, grad_factor, value_factor, counts, row_token):
    n_dp, n_exp, across, queries, real_cols, granule = dims
    gfac, vfac = grad_factor[0].T, value_factor[0].T
    cols = round_up(real_cols, PACK)
    if cols != real_cols:
        pad = ((0, cols - real_cols), (0, 0))
        gfac, vfac = jnp.pad(gfac, pad), jnp.pad(vfac, pad)
    slots, model = row_acts.shape[1:]
    units = row_grads.shape[2]
    width = units + model
    chips = n_dp // 2
    steps = chips // 2
    depth = round_up(queries + 1, 8)
    n_tok = n_exp * TOK_DEV
    edge = n_exp // 2 * TOK_DEV
    n_pieces = 1 + len(V_EIGHTHS)
    few = real_cols // RANK if real_cols % RANK == 0 else (real_cols - 1) // RANK + 2
    any_space = pl.BlockSpec(memory_space=pl.ANY)
    turned = pl.pallas_call(
        functools.partial(kernel, (*dims, units)),
        name="influence_exchange",
        out_shape=pltpu.VMEM((queries, TOK_DEV), jnp.float32),
        in_specs=[pl.BlockSpec(memory_space=pltpu.SMEM)] + [any_space] * 5,
        out_specs=pl.BlockSpec(memory_space=pltpu.VMEM),
        scratch_shapes=[
            pltpu.VMEM((1, slots), jnp.int32),
            pltpu.VMEM((slots, width), jnp.bfloat16),
            pltpu.VMEM((n_tok, width), jnp.bfloat16),
            pltpu.VMEM((edge, width), jnp.bfloat16),
            pltpu.VMEM((n_dp, cols, width), jnp.bfloat16),
            pltpu.VMEM((2, 2, cols, n_tok), jnp.float32),
            pltpu.VMEM((2, 2, cols, n_tok), jnp.float32),
            pltpu.VMEM((2, cols, edge), jnp.float32),
            pltpu.VMEM((2, cols, edge), jnp.float32),
            pltpu.VMEM((depth, n_tok), jnp.float32),
            pltpu.VMEM((n_tok, slots), jnp.bfloat16),
            pltpu.VMEM((2, n_tok, LANES), jnp.float32),
            pltpu.VMEM((n_exp, depth, TOK_DEV), jnp.float32),
            pltpu.VMEM((n_exp, 2, few, 1, TOK_DEV), jnp.float32),
            pltpu.VMEM((n_exp, 2, few, 1, TOK_DEV), jnp.float32),
            pltpu.SemaphoreType.DMA((3,)),
            pltpu.SemaphoreType.DMA((1,)),
            pltpu.SemaphoreType.DMA((1,)),
            pltpu.SemaphoreType.DMA((steps, n_pieces)),
            pltpu.SemaphoreType.DMA((steps, n_pieces)),
            pltpu.SemaphoreType.DMA((4,)),
            pltpu.SemaphoreType.DMA((2,)),
            pltpu.SemaphoreType.DMA((2,)),
        ],
        compiler_params=pltpu.CompilerParams(
            collective_id=0, has_side_effects=True, vmem_limit_bytes=60 * 1024 * 1024
        ),
    )(counts, row_token, row_acts[0], row_grads[0], gfac, vfac)
    return turned.T


def solution(mesh):
    n_exp, n_dp = mesh.shape["expert"], mesh.shape["dp"]
    across = len({d.coords[0] for d in mesh.devices.flat})

    def whole(row_acts, row_grads, grad_factor, value_factor, counts, row_token):
        all_cols = grad_factor.shape[2]
        real_cols = all_cols // n_dp
        granule = real_cols if RANK % real_cols == 0 else RANK
        while real_cols % granule:
            granule //= 2
        dims = (n_dp, n_exp, across, all_cols // RANK, real_cols, granule)
        return jax.shard_map(
            functools.partial(local, dims),
            mesh=mesh,
            in_specs=(
                P("expert", "dp", None),
                P("expert", "dp", None),
                P("expert", None, "dp"),
                P("expert", None, "dp"),
                P("expert", "dp"),
                P("expert", "dp"),
            ),
            out_specs=P(("expert", "dp"), None),
            check_vma=False,
        )(row_acts, row_grads, grad_factor, value_factor, counts, row_token)

    return whole
```

```python
import functools

import jax
import jax.numpy as jnp
from jax import lax
from jax.experimental import pallas as pl
from jax.experimental.pallas import tpu as pltpu
from jax.sharding import PartitionSpec as P

RANK = 32
TOK_DEV = 256
LANES = 128
PACK = 16
V_EIGHTHS = (3, 2, 2, 1)
CHUNK = 256
CHUNKS_BEFORE_RELAY = 8

epsilon = 1e-06
MESH = pl.DeviceIdType.MESH
CONTRACT_LAST = (((1,), (1,)), ((), ()))


def round_up(value, unit):
    return -(-value // unit) * unit


def kernel(
    dims,
    count_ref,
    token_hbm,
    acts_hbm,
    grads_hbm,
    gfac_hbm,
    vfac_hbm,
    out_ref,
    tokens,
    rows,
    by_token,
    mate,
    fac,
    gproj,
    aproj,
    edge_g,
    edge_a,
    scores,
    onehot,
    energies,
    landed,
    far_dense,
    far_landed,
    load_sem,
    send_sem,
    own_sem,
    direct_sem,
    relay_sem,
    mate_sem,
    zsend_sem,
    zrecv_sem,
):
    n_dp, n_exp, across, queries, real_cols, granule, units = dims
    chips = n_dp // 2
    half = chips // 2
    slots, width = rows.shape
    model = width - units
    n_tok = by_token.shape[0]
    cols = fac.shape[1]
    me_e = lax.axis_index("expert")
    me = lax.axis_index("dp")
    core = me % 2
    other = 1 - core

    def walk(index):
        line, at = index // across, index % across
        back = line % 2
        return line * across + at + back * (across - 1 - 2 * at)

    place = walk(me // 2)

    def chip_at(step):
        return walk((place + step + chips) % chips)

    mine = chip_at(0)
    ahead = chip_at(1) * 2 + core
    behind = chip_at(-1) * 2 + core
    partner = mine * 2 + other

    pieces, start = [pl.ds(0, units)], units
    for part in V_EIGHTHS:
        pieces.append(pl.ds(start, part * model // 8))
        start += part * model // 8
    n_pieces = len(pieces)
    last_piece = n_pieces - 1
    joined = pl.ds(pieces[-2].start, pieces[-2].size + pieces[-1].size)
    coarse = pieces[:-2] + [joined]

    def piece_of(step, j):
        return pieces[j] if step == half else coarse[j]


    def own(j):
        if j == 0:
            return gfac_hbm
        return vfac_hbm.at[:, pl.ds(pieces[j].start - units, pieces[j].size)]

    sent = []

    def send(src, dst, sem, target):
        copy = pltpu.make_async_remote_copy(
            src_ref=src,
            dst_ref=dst,
            send_sem=send_sem.at[0],
            recv_sem=sem,
            device_id=(me_e, target),
            device_id_type=MESH,
        )
        copy.start()
        sent.append(src.shape[0] * src.shape[1])

    def wait_for(ref, sem):
        pltpu.make_async_remote_copy(
            src_ref=ref,
            dst_ref=ref,
            send_sem=send_sem.at[0],
            recv_sem=sem,
            device_id=(me_e, partner),
            device_id_type=MESH,
        ).wait_recv()

    barrier = pltpu.get_barrier_semaphore()
    for target in (ahead, behind, partner):
        pl.semaphore_signal(barrier, inc=1, device_id=(me_e, target), device_id_type=MESH)
    for i in range(1, n_exp):
        pl.semaphore_signal(
            barrier, inc=1, device_id=((me_e + i) % n_exp, me), device_id_type=MESH
        )

    g_span, v_span = pl.ds(0, units), pl.ds(units, model)
    own_slot = mine * 2 + core
    load_tokens = pltpu.make_async_copy(token_hbm, tokens, load_sem.at[0])
    load_tokens.start()
    pltpu.make_async_copy(gfac_hbm, fac.at[own_slot, :, g_span], load_sem.at[2]).start()
    pltpu.make_async_copy(vfac_hbm, fac.at[own_slot, :, v_span], load_sem.at[2]).start()
    pltpu.make_async_copy(grads_hbm, rows.at[:, g_span], load_sem.at[1]).start()
    pltpu.make_async_copy(acts_hbm, rows.at[:, v_span], load_sem.at[1]).start()
    with jax.named_scope("barrier"):
        pl.semaphore_wait(barrier, 3 + n_exp - 1)

    own_shard = fac.at[own_slot]
    pltpu.make_async_copy(own_shard, own_shard, load_sem.at[2]).wait()
    for j in range(len(coarse)):
        for target in (ahead, behind):
            part = fac.at[own_slot, :, coarse[j]]
            send(part, part, direct_sem.at[0, j], target)
    send(own_shard, own_shard, own_sem.at[0], partner)

    with jax.named_scope("onehot"):
        load_tokens.wait()
        slot_ids = lax.broadcasted_iota(jnp.int32, (1, slots), 1)
        names = jnp.where(slot_ids < count_ref[0, 0], tokens[...], -1)
        token_ids = lax.broadcasted_iota(jnp.int32, onehot.shape, 0)
        onehot[...] = (token_ids == names).astype(jnp.float32).astype(onehot.dtype)
        scores[...] = jnp.zeros_like(scores)
        far_dense[...] = jnp.zeros_like(far_dense)
        energies[...] = jnp.zeros_like(energies)

    with jax.named_scope("loadwait"):
        pltpu.make_async_copy(rows, rows, load_sem.at[1]).wait()

    def order_rows(first, size):
        part = jnp.dot(
            onehot[...], rows[:, first : first + size], preferred_element_type=jnp.float32
        )
        by_token[:, first : first + size] = part.astype(by_token.dtype)
        kind = int(first >= units)
        squares = part * part
        for i in range(size // LANES):
            energies[kind] += squares[:, i * LANES : (i + 1) * LANES]

    chunks = [(i, CHUNK) for i in range(0, width, CHUNK)]

    def project(factor, ref, span):
        return lax.dot_general(
            factor, ref[:, span], CONTRACT_LAST, preferred_element_type=jnp.float32
        )

    def project_pair(sources, span):
        factor = [fac[pl.ds(2 * chip, 2), :, span] for chip in sources]
        factor = jnp.concatenate([f.reshape(2 * cols, span.size) for f in factor], axis=0)
        return project(factor, by_token, span).reshape(len(sources), 2, cols, n_tok)

    def group_sums(chip, side, product):
        for i in range(real_cols // granule):
            query = ((2 * chip + side) * real_cols + i * granule) // RANK
            part = product[i * granule : (i + 1) * granule]
            yield query, jnp.sum(part, axis=0, keepdims=True)

    def owner_at(k):
        low = k + (k >= me_e).astype(jnp.int32)
        high = n_exp - 1 - k
        high = high - (high <= me_e).astype(jnp.int32)
        return jnp.where(2 * me_e < n_exp, high, low)

    def of_owner(owner):
        return pl.ds(pl.multiple_of(owner * TOK_DEV, TOK_DEV), TOK_DEV)

    def hand_over(stage, src, dst, owner, target=me):
        pltpu.make_async_remote_copy(
            src_ref=src,
            dst_ref=dst,
            send_sem=zsend_sem.at[stage],
            recv_sem=zrecv_sem.at[stage],
            device_id=(owner, target),
            device_id_type=MESH,
        ).start()

    def handed(stage, all_of):
        return pltpu.make_async_remote_copy(
            src_ref=all_of,
            dst_ref=all_of,
            send_sem=zsend_sem.at[stage],
            recv_sem=zrecv_sem.at[stage],
            device_id=((me_e + 1) % n_exp, me),
            device_id_type=MESH,
        )

    def sources_of(step):
        return [chip_at(-step)] if step == half else [chip_at(-step), chip_at(step)]

    def pass_on(step, j):
        sources = sources_of(step)
        count = len(sources)
        span = piece_of(step, j)
        wait_for(fac.at[pl.ds(0, count), :, span], direct_sem.at[step - 1, j])

        def relay(chip, sem, target, span=span):
            part = fac.at[2 * chip + core, :, span]
            send(part, part, sem, target)

        if step < half - 1:
            relay(sources[0], direct_sem.at[step, j], ahead)
            relay(sources[1], direct_sem.at[step, j], behind)
        elif step == half - 1:
            chip = chip_at(step * (2 * core - 1))
            target = chip_at(1 - 2 * core) * 2 + core
            for i in range(j, n_pieces if j == len(coarse) - 1 else j + 1):
                relay(chip, direct_sem.at[step, i], target, pieces[i])
        for chip in sources:
            relay(chip, relay_sem.at[step - 1, j], partner)

    def relayed(step, j):
        count = len(sources_of(step))
        wait_for(fac.at[pl.ds(0, count), :, piece_of(step, j)], relay_sem.at[step - 1, j])

    far_chip = chip_at(half)

    def base_of(side):
        return (2 * far_chip + side) * real_cols // RANK

    def multiply(step, j):
        sources = sources_of(step)
        count = len(sources)
        relayed(step, j)
        value = project_pair(sources, piece_of(step, j))
        if j == 0:
            gproj[:count] = value
        elif j == 1:
            aproj[:count] = value
        elif j < len(coarse) - 1:
            aproj[:count] += value
        else:
            product = (aproj[:count] + value) * gproj[:count]
            for buf, chip in enumerate(sources):
                for side in range(2):
                    for query, total in group_sums(chip, side, product[buf, side]):
                        scores[pl.ds(query, 1)] += total

    edge = mate.shape[0]
    lower = 2 * me_e < n_exp
    edge_start = pl.multiple_of(jnp.where(lower, n_tok - edge, 0), TOK_DEV)
    rest_start = pl.multiple_of(jnp.where(lower, 0, edge), TOK_DEV)
    edge_tok, rest = pl.ds(edge_start, edge), pl.ds(rest_start, n_tok - edge)
    middle = pieces[3].start
    mate_spans = [
        g_span, pl.ds(units, middle - units), pl.ds(middle, width - middle)
    ]

    def lend(part):
        span = mate_spans[part]
        pltpu.make_async_remote_copy(
            src_ref=by_token.at[edge_tok, span],
            dst_ref=mate.at[:, span],
            send_sem=mate_sem.at[3],
            recv_sem=mate_sem.at[part],
            device_id=(me_e, partner),
            device_id_type=MESH,
        ).start()

    with jax.named_scope("perm"):
        for at, chunk in enumerate(chunks):
            order_rows(*chunk)
            for part in range(2):
                if chunk[0] == mate_spans[part + 1].start:
                    lend(part)
            if at == CHUNKS_BEFORE_RELAY - 1:
                with jax.named_scope("pass10"):
                    pass_on(1, 0)
    with jax.named_scope("energy"):
        totals = [
            jnp.sum(energies[kind].T, axis=0, keepdims=True) for kind in range(2)
        ]
        scores[queries : queries + 1] = totals[0] * totals[1]
    lend(2)

    with jax.named_scope("mineg"):
        own_shard = fac.at[own_slot]
        wait_for(own_shard, own_sem.at[0])
        gproj[0] = project_pair([mine], g_span)[0]
    with jax.named_scope("pass11"):
        pass_on(1, 1)
    with jax.named_scope("minev"):
        product = project_pair([mine], v_span)[0] * gproj[0]
        for side in range(2):
            for query, total in group_sums(mine, side, product[side]):
                scores[pl.ds(query, 1)] += total

    def edge_product(j):
        for part, span in enumerate(mate_spans):
            if pieces[j].start == span.start:
                wait_for(mate.at[:, span], mate_sem.at[part])
        factor = fac[2 * far_chip + core, :, pieces[j]]
        both = jnp.concatenate([by_token[edge_tok, pieces[j]], mate[:, pieces[j]]], axis=0)
        value = lax.dot_general(
            factor, both, CONTRACT_LAST, preferred_element_type=jnp.float32
        )
        return [value[:, :edge], value[:, edge:]]

    def edge_multiply(j):
        for kind, part in enumerate(edge_product(j)):
            if j == 0:
                edge_g[kind] = part
            elif j == 1:
                edge_a[kind] = part
            else:
                edge_a[kind] += part

    def rest_product(j):
        factor = fac[pl.ds(2 * far_chip, 2), :, pieces[j]]
        factor = factor.reshape(2 * cols, pieces[j].size)
        value = project(factor, by_token.at[rest], pieces[j])
        return value.reshape(2, cols, n_tok - edge)

    def rest_multiply(j):
        relayed(half, j)
        value = rest_product(j)
        if j == 0:
            gproj[0, :, :, rest] = value
        elif j == 1:
            aproj[0, :, :, rest] = value
        else:
            aproj[0, :, :, rest] += value

    order = [(step, j) for step in range(1, half) for j in range(len(coarse))]
    for at, event in enumerate(order):
        if at > 1:
            with jax.named_scope(f"pass{event[0]}{event[1]}"):
                pass_on(*event)
        if at:
            with jax.named_scope(f"mul{order[at - 1][0]}{order[at - 1][1]}"):
                multiply(*order[at - 1])
    with jax.named_scope("mullast"):
        multiply(*order[-1])
    with jax.named_scope("near"):
        for k in range(n_exp - 1):
            owner = owner_at(k)
            hand_over(0, scores.at[:, of_owner(owner)], landed.at[me_e], owner)
    for j in range(last_piece):
        with jax.named_scope(f"pass{half}{j}"):
            pass_on(half, j)
        with jax.named_scope(f"edge{j}"):
            edge_multiply(j)
        if 1 < j < last_piece - 1:
            with jax.named_scope(f"rest{j - 2}"):
                rest_multiply(j - 2)
    with jax.named_scope(f"pass{half}{last_piece}"):
        pass_on(half, last_piece)

    def far_sums(kind, side, product, first, count):
        for query, total in group_sums(far_chip, side, product):
            for i in range(count):
                far_dense[first + i, kind, query - base_of(side)] += total[
                    :, i * TOK_DEV : (i + 1) * TOK_DEV
                ]

    n_edge = edge // TOK_DEV
    edge_first = jnp.where(lower, n_exp - n_edge, 0)
    rest_first = jnp.where(lower, 0, n_edge)
    with jax.named_scope("edge"):
        for kind, value in enumerate(edge_product(last_piece)):
            product = (edge_a[kind] + value) * edge_g[kind]
            far_sums(kind, core, product, edge_first, n_edge)
            for k in range(n_edge):
                hand_over(
                    1,
                    far_dense.at[owner_at(k), kind],
                    far_landed.at[me_e, core],
                    owner_at(k),
                    partner if kind else me,
                )
    for j in range(last_piece - 3, last_piece):
        with jax.named_scope(f"rest{j}"):
            rest_multiply(j)
    with jax.named_scope("lastrelay"):
        relayed(half, last_piece)
    with jax.named_scope("far"):
        value = rest_product(last_piece)
        for side in range(2):
            product = (aproj[0, side, :, rest] + value[side]) * gproj[0, side, :, rest]
            far_sums(side, side, product, rest_first, n_exp - n_edge)
        for k in range(n_edge, n_exp - 1):
            owner = owner_at(k)
            hand_over(1, far_dense.at[owner], far_landed.at[me_e], owner)

    with jax.named_scope("colnear"):
        result = scores[:, of_owner(me_e)]
        near_wait = handed(0, landed.at[pl.ds(0, n_exp - 1)])
        near_wait.wait_recv()
        for k in range(n_exp - 1):
            result = result + landed[owner_at(k)]
        factor = lax.rsqrt(result[queries : queries + 1] / (model * units) + epsilon)
        factor = factor / jnp.sqrt(jnp.float32(RANK))
    with jax.named_scope("colfar"):
        far_wait = handed(1, far_landed.at[pl.ds(0, n_exp - 1)])
        far_wait.wait_recv()
    late = far_dense[me_e]
    for k in range(n_exp - 1):
        late = late + far_landed[owner_at(k)]
    row_ids = lax.broadcasted_iota(jnp.int32, result.shape, 0)
    for side in range(2):
        for i in range(late.shape[1]):
            row = row_ids == base_of(side) + i
            result = result + jnp.where(row, late[side, i], 0.0)
    out_ref[...] = result[:queries] * factor
    with jax.named_scope("sends"):
        near_wait.wait_send()
        far_wait.wait_send()

        def sent_all(ref, sem):
            pltpu.make_async_remote_copy(
                src_ref=ref,
                dst_ref=ref,
                send_sem=sem,
                recv_sem=own_sem.at[0],
                device_id=(me_e, partner),
                device_id_type=MESH,
            ).wait_send()

        sent_all(mate, mate_sem.at[3])
        sent_all(fac.at[pl.ds(0, sum(sent) // (cols * width))], send_sem.at[0])


def local(dims, row_acts, row_grads, grad_factor, value_factor, counts, row_token):
    n_dp, n_exp, across, queries, real_cols, granule = dims
    gfac, vfac = grad_factor[0].T, value_factor[0].T
    cols = round_up(real_cols, PACK)
    if cols != real_cols:
        pad = ((0, cols - real_cols), (0, 0))
        gfac, vfac = jnp.pad(gfac, pad), jnp.pad(vfac, pad)
    slots, model = row_acts.shape[1:]
    units = row_grads.shape[2]
    width = units + model
    chips = n_dp // 2
    steps = chips // 2
    depth = round_up(queries + 1, 8)
    n_tok = n_exp * TOK_DEV
    edge = n_exp // 2 * TOK_DEV
    n_pieces = 1 + len(V_EIGHTHS)
    few = real_cols // RANK if real_cols % RANK == 0 else (real_cols - 1) // RANK + 2
    any_space = pl.BlockSpec(memory_space=pl.ANY)
    turned = pl.pallas_call(
        functools.partial(kernel, (*dims, units)),
        name="influence_exchange",
        out_shape=pltpu.VMEM((queries, TOK_DEV), jnp.float32),
        in_specs=[pl.BlockSpec(memory_space=pltpu.SMEM)] + [any_space] * 5,
        out_specs=pl.BlockSpec(memory_space=pltpu.VMEM),
        scratch_shapes=[
            pltpu.VMEM((1, slots), jnp.int32),
            pltpu.VMEM((slots, width), jnp.bfloat16),
            pltpu.VMEM((n_tok, width), jnp.bfloat16),
            pltpu.VMEM((edge, width), jnp.bfloat16),
            pltpu.VMEM((n_dp, cols, width), jnp.bfloat16),
            pltpu.VMEM((2, 2, cols, n_tok), jnp.float32),
            pltpu.VMEM((2, 2, cols, n_tok), jnp.float32),
            pltpu.VMEM((2, cols, edge), jnp.float32),
            pltpu.VMEM((2, cols, edge), jnp.float32),
            pltpu.VMEM((depth, n_tok), jnp.float32),
            pltpu.VMEM((n_tok, slots), jnp.bfloat16),
            pltpu.VMEM((2, n_tok, LANES), jnp.float32),
            pltpu.VMEM((n_exp, depth, TOK_DEV), jnp.float32),
            pltpu.VMEM((n_exp, 2, few, 1, TOK_DEV), jnp.float32),
            pltpu.VMEM((n_exp, 2, few, 1, TOK_DEV), jnp.float32),
            pltpu.SemaphoreType.DMA((3,)),
            pltpu.SemaphoreType.DMA((1,)),
            pltpu.SemaphoreType.DMA((1,)),
            pltpu.SemaphoreType.DMA((steps, n_pieces)),
            pltpu.SemaphoreType.DMA((steps, n_pieces)),
            pltpu.SemaphoreType.DMA((4,)),
            pltpu.SemaphoreType.DMA((2,)),
            pltpu.SemaphoreType.DMA((2,)),
        ],
        compiler_params=pltpu.CompilerParams(
            collective_id=0, has_side_effects=True, vmem_limit_bytes=60 * 1024 * 1024
        ),
    )(counts, row_token, row_acts[0], row_grads[0], gfac, vfac)
    return turned.T


def solution(mesh):
    n_exp, n_dp = mesh.shape["expert"], mesh.shape["dp"]
    across = len({d.coords[0] for d in mesh.devices.flat})

    def whole(row_acts, row_grads, grad_factor, value_factor, counts, row_token):
        all_cols = grad_factor.shape[2]
        real_cols = all_cols // n_dp
        granule = real_cols if RANK % real_cols == 0 else RANK
        while real_cols % granule:
            granule //= 2
        dims = (n_dp, n_exp, across, all_cols // RANK, real_cols, granule)
        return jax.shard_map(
            functools.partial(local, dims),
            mesh=mesh,
            in_specs=(
                P("expert", "dp", None),
                P("expert", "dp", None),
                P("expert", None, "dp"),
                P("expert", None, "dp"),
                P("expert", "dp"),
                P("expert", "dp"),
            ),
            out_specs=P(("expert", "dp"), None),
            check_vma=False,
        )(row_acts, row_grads, grad_factor, value_factor, counts, row_token)

    return whole
```
